128 devices in a mesh: lat: 8 (over y, core), lon: 16 (over z, x).
Axes of the slice: x: 4, y: 4, z: 4, core: 2. Of those that a mesh axis runs over, the one named last changes fastest.
Arguments:
- temp: float32 [64, 256, 2048], P(None, 'lat', 'lon'), may hold values from -6 to 6
- salt: float32 [64, 256, 2048], P(None, 'lat', 'lon'), may hold values from -6 to 6
- u_east: float32 [64, 256, 2048], P(None, 'lat', 'lon'), may hold values from -1.2 to 1.2
- v_north: float32 [64, 256, 2048], P(None, 'lat', 'lon'), may hold values from -1.2 to 1.2
- vdiff: float32 [64, 256, 2048], P(None, 'lat', 'lon'), may hold values from 0.05 to 5
- kmt: int32 [256, 2048], P('lat', 'lon'), may hold values from 0 to 64
- owner: int32 [4, 256, 2048], P(None, 'lat', 'lon'), may hold values from 0 to 127, as said below
- atmo_cell: int32 [4, 256, 2048], P(None, 'lat', 'lon'), may hold values from 0 to 2047
- weight: float32 [4, 256, 2048], P(None, 'lat', 'lon'), may hold values from 0.01 to 0.06
Outputs:
- temp_out: float32 [64, 256, 2048], P(None, 'lat', 'lon')
- salt_out: float32 [64, 256, 2048], P(None, 'lat', 'lon')
- atmo_fields: float32 [2, 262144], P(None, ('lat', 'lon'))
The draws below stay inside these ranges and needn't reach their ends.
Inputs may be any that keep to these rules, and one draw needn't show every extreme that they name: Within each device's block of 32 x 128 ocean cells (all 4 links of a cell together) no owner is named by more than 512 links; in every draw one owner is named by exactly 512 links of every device's block.
All inputs are finite; a program needn't handle non-finite values.
Results may differ from the reference program's by a relative error of at most 0.00011.
Values sent between devices are 32-bit elements; how exact they have to be, the bound alone decides.
A program may use at most 128 MiB of HBM per device.

```python
import math
import jax
import jax.numpy as jnp

K = 64
CJ = 32
CI = 128
LINKS = 4
A_DEV = 2048
STEPS = 2
NYG = 256
NXG = 2048
ATMO = 262144
CAP = 512
N_LAT = 8
N_LON = 16
DEVICES = 128


def draw_owner(key, part):
    links_dev = LINKS * CJ * CI
    key_hot, key_second, key_extra, key_perm, key_turn = jax.random.split(jax.random.fold_in(key, 17), 5)
    hottest = jax.random.randint(key_hot, (), 0, DEVICES)
    spread_most = (links_dev - CAP + DEVICES - 2) // (DEVICES - 1)
    second = (hottest + 1 + jax.random.randint(key_second, (DEVICES,), 0, DEVICES - 1)) % DEVICES
    extra = jax.random.randint(key_extra, (DEVICES,), 0, CAP - spread_most + 1)
    turned = jax.random.randint(key_turn, (DEVICES,), 0, DEVICES - 1)
    ranks = jax.vmap(lambda single: jax.random.permutation(single, links_dev))(jax.random.split(key_perm, DEVICES))
    leftover = ranks - CAP - extra[:, None]
    others = (hottest + 1 + (leftover + turned[:, None]) % (DEVICES - 1)) % DEVICES
    chosen = jnp.where(ranks < CAP, hottest, jnp.where(ranks < CAP + extra[:, None], second[:, None], others))
    shaped = chosen.reshape(N_LAT, N_LON, LINKS, CJ, CI).transpose(2, 0, 3, 1, 4)
    return shaped.reshape(LINKS, NYG, NXG).astype(jnp.int32)


def set_ends(values, own_key, smallest, top_value):
    longest = values.shape.index(max(values.shape))
    spots = []
    for shift in (0, 1):
        where = [jax.random.randint(jax.random.fold_in(own_key, axis), (), 0, length) for axis, length in enumerate(values.shape)]
        where[longest] = (where[longest] + shift) % values.shape[longest]
        spots.append(tuple(where))
    return values.at[spots[0]].set(smallest).at[spots[1]].set(top_value)


def shard_levels(own_key, extent, pieces, smallest, high):
    gain = 1.0
    for axis_at, blocks in pieces:
        steps = jax.random.uniform(jax.random.fold_in(jax.random.fold_in(own_key, 6), axis_at), (blocks,), jnp.float32, smallest / len(pieces), high / len(pieces))
        gain = gain * jnp.repeat(jnp.exp(steps), extent[axis_at] // blocks).reshape((-1,) + (1,) * (len(extent) - 1 - axis_at))
    return gain


def normal_values(rng, shape, width, bound, cuts=(), kind=jnp.bfloat16):
    values = width * jax.random.normal(rng, shape, jnp.float32)
    if cuts:
        values = values * shard_levels(rng, shape, cuts, -0.22, 0.18)
    return jnp.clip(values, -bound, bound).astype(kind)


def setup_inputs(seed: int = 0) -> dict:
    key_list = jax.random.split(jax.random.key(seed), 10)
    temp = normal_values(key_list[0], (K, NYG, NXG), 1.0, 6.0, ((1, 8), (2, 16)), jnp.float32)
    salt = normal_values(key_list[1], (K, NYG, NXG), 1.0, 6.0, ((1, 8), (2, 16)), jnp.float32)
    u_east = normal_values(key_list[2], (K, NYG, NXG), 0.2, 1.2, ((1, 8), (2, 16)), jnp.float32)
    v_north = normal_values(key_list[3], (K, NYG, NXG), 0.2, 1.2, ((1, 8), (2, 16)), jnp.float32)
    vdiff = jnp.clip(jnp.exp(math.log(5.0) - 4.6051702 * jax.random.uniform(key_list[4], (K, NYG, NXG), jnp.float32) ** shard_levels(key_list[4], (K, NYG, NXG), ((1, 8), (2, 16)), -0.2, 0.2)), 0.05, 5.0)
    kmt = set_ends(jax.random.randint(key_list[5], (NYG, NXG), 0, K + 1), jax.random.fold_in(key_list[5], 1), 0, K).astype(jnp.int32)
    owner = draw_owner(jax.random.fold_in(key_list[9], 71), 0)
    atmo_cell = set_ends(jax.random.randint(key_list[7], (LINKS, NYG, NXG), 0, A_DEV), jax.random.fold_in(key_list[7], 1), 0, A_DEV - 1).astype(jnp.int32)
    weight = jnp.clip(0.01 + 0.04999999888241291 * jax.random.uniform(key_list[8], (LINKS, NYG, NXG), jnp.float32) ** shard_levels(key_list[8], (LINKS, NYG, NXG), ((1, 8), (2, 16)), -0.2, 0.2), 0.01, 0.06)
    return {"temp": temp, "salt": salt, "u_east": u_east, "v_north": v_north, "vdiff": vdiff, "kmt": kmt, "owner": owner, "atmo_cell": atmo_cell, "weight": weight}


mixing = 0.1


def lon_pad(field):
    return jnp.concatenate([field[..., -1:], field, field[..., :1]], axis=-1)


def fold_pad(field):
    wrapped = lon_pad(field)
    south_row = jnp.zeros_like(wrapped[..., :1, :])
    north_row = lon_pad(jnp.flip(field[..., -1:, :], axis=-1))
    return jnp.concatenate([south_row, wrapped, north_row], axis=-2)


def vertical_solve(moved, wet_mask, vdiff):
    depth_count = moved.shape[1]
    zero_plane = jnp.zeros_like(vdiff[0])
    coupling = [vdiff[level_idx] * wet_mask[level_idx + 1] for level_idx in range(depth_count - 1)]
    ratios = []
    forward = []
    for level_idx in range(depth_count):
        upper_c = coupling[level_idx] if level_idx < depth_count - 1 else zero_plane
        lower_c = coupling[level_idx - 1] if level_idx > 0 else zero_plane
        diagonal = 1.0 + lower_c + upper_c
        if level_idx == 0:
            denominator = diagonal
            solved = moved[:, 0] / denominator
        else:
            denominator = diagonal + lower_c * ratios[-1]
            solved = (moved[:, level_idx] + lower_c * forward[-1]) / denominator
        ratios.append(-upper_c / denominator)
        forward.append(solved)
    result = [None] * depth_count
    result[-1] = forward[-1]
    for level_idx in range(depth_count - 2, -1, -1):
        result[level_idx] = forward[level_idx] - ratios[level_idx] * result[level_idx + 1]
    return jnp.stack(result, axis=1)


def tracer_update(tracer_pad, mask_pad, east_pad, north_pad, wet_mask, vdiff):
    mask_east = mask_pad[:, 1:-1, :-1] * mask_pad[:, 1:-1, 1:]
    mask_north = mask_pad[:, :-1, 1:-1] * mask_pad[:, 1:, 1:-1]
    east_face = east_pad[:, 1:-1, :-1]
    north_face = north_pad[:, :-1, 1:-1]
    west_side = tracer_pad[:, :, 1:-1, :-1]
    east_side = tracer_pad[:, :, 1:-1, 1:]
    flux_east = mask_east * (east_face * 0.5 * (west_side + east_side) - mixing * (east_side - west_side))
    south_side = tracer_pad[:, :, :-1, 1:-1]
    north_side = tracer_pad[:, :, 1:, 1:-1]
    flux_north = mask_north * (north_face * 0.5 * (south_side + north_side) - mixing * (north_side - south_side))
    centre = tracer_pad[:, :, 1:-1, 1:-1]
    spread = flux_east[..., 1:] - flux_east[..., :-1] + flux_north[..., 1:, :] - flux_north[..., :-1, :]
    moved = centre - wet_mask * spread
    return vertical_solve(moved, wet_mask, vdiff)


def reference(temp, salt, u_east, v_north, vdiff, kmt, owner, atmo_cell, weight):
    level_ids = jnp.arange(K, dtype=jnp.int32)[:, None, None]
    wet_mask = (level_ids < kmt[None]).astype(jnp.float32)
    mask_pad = fold_pad(wet_mask)
    east_pad = fold_pad(u_east)
    north_pad = fold_pad(v_north)
    tracers = jnp.stack([temp, salt])
    for step_idx in range(STEPS):
        tracers = tracer_update(fold_pad(tracers), mask_pad, east_pad, north_pad, wet_mask, vdiff)
    surface = tracers[:, 0] * wet_mask[0]
    values = (weight[None] * surface[:, None]).reshape(2, -1)
    target = (owner * A_DEV + atmo_cell).reshape(-1).astype(jnp.int32)
    atmo_t = jax.ops.segment_sum(values[0], target, num_segments=ATMO)
    atmo_s = jax.ops.segment_sum(values[1], target, num_segments=ATMO)
    return tracers[0], tracers[1], jnp.stack([atmo_t, atmo_s])
```

```python
import functools

import jax
import jax.numpy as jnp
from jax import lax
from jax.experimental import pallas as pl
from jax.experimental.pallas import tpu as pltpu
from jax.sharding import PartitionSpec as P


I32 = jnp.int32
F32 = jnp.float32


def lanes_of(x, idx):
    return jnp.take_along_axis(x, idx, axis=1, mode="promise_in_bounds")


def subs_of(x, idx):
    return jnp.take_along_axis(x, idx, axis=0, mode="promise_in_bounds")


def sort_links(keys, loads):
    lane = lax.broadcasted_iota(I32, (8, 128), 1)
    sub = lax.broadcasted_iota(I32, (8, 128), 0)
    lane_swap = [lane ^ (1 << b) for b in range(7)]
    sub_swap = [sub ^ (1 << b) for b in range(3)]

    def bit(b):
        if b < 4:
            return None
        if b < 7:
            return ((sub >> (b - 4)) & 1) == 1
        if b < 14:
            return ((lane >> (b - 7)) & 1) == 1
        return None

    for top in range(1, 15):
        for b in range(top - 1, -1, -1):
            down = bit(top)
            if b < 4:
                new_k, new_w = list(keys), list(loads)
                for v in range(16):
                    if (v >> b) & 1:
                        continue
                    u = v | (1 << b)
                    swap = keys[v] > keys[u]
                    if top < 4:
                        if (v >> top) & 1:
                            swap = keys[v] < keys[u]
                    elif down is not None:
                        swap = jnp.logical_xor(swap, down)
                    new_k[v] = jnp.where(swap, keys[u], keys[v])
                    new_k[u] = jnp.where(swap, keys[v], keys[u])
                    new_w[v] = jnp.where(swap, loads[u], loads[v])
                    new_w[u] = jnp.where(swap, loads[v], loads[u])
                keys, loads = new_k, new_w
            else:
                high = bit(b)
                keep_max = high if down is None else jnp.logical_xor(high, down)
                if b < 7:
                    fetch = functools.partial(subs_of, idx=sub_swap[b - 4])
                else:
                    fetch = functools.partial(lanes_of, idx=lane_swap[b - 7])
                new_k, new_w = [], []
                for v in range(16):
                    k, w = keys[v], loads[v]
                    pk, pw = fetch(k), fetch(w)
                    more, less = pk > k, pk < k
                    take = jnp.logical_or(
                        jnp.logical_and(keep_max, more),
                        jnp.logical_and(jnp.logical_not(keep_max), less),
                    )
                    new_k.append(jnp.where(take, pk, k))
                    new_w.append(jnp.where(take, pw, w))
                keys, loads = new_k, new_w
    return keys, loads


def owner_starts(keys):
    lane = lax.broadcasted_iota(I32, (8, 128), 1)
    first = jnp.broadcast_to(keys[0][0:1, :], (8, 128))
    bound = lane << 23
    count = jnp.zeros((8, 128), I32)
    for step in (128, 64, 32, 16, 8, 4, 2, 1):
        trial = count + step
        value = lanes_of(first, jnp.minimum(trial - 1, 127))
        fits = jnp.logical_and(trial <= 128, value < bound)
        count = jnp.where(fits, trial, count)
    column = jnp.maximum(count - 1, 0)
    within = jnp.zeros((8, 128), I32)
    for v in range(16):
        within = within + jnp.where(lanes_of(keys[v], column) < bound, 1, 0)
    within = jnp.broadcast_to(jnp.sum(within, axis=0, keepdims=True), (8, 128))
    return jnp.where(count > 0, column * 128 + within, 0)


def owner_slots(tiles, start):
    sub = lax.broadcasted_iota(I32, (8, 128), 0)
    column = start >> 7
    turn = start & 127
    x = []
    for c in range(5):
        idx = jnp.minimum(column + c, 127)
        x.append([lanes_of(tiles[v], idx) for v in range(16)])
    for n in (64, 32, 16):
        on = (turn & n) != 0
        a = n // 16
        low = sub < 8 - a
        rolled = [[pltpu.roll(t, 8 - a, 0) for t in row] for row in x]
        x = [
            [
                jnp.where(on, jnp.where(low, rolled[c][v], rolled[min(c + 1, 4)][v]), x[c][v])
                for v in range(16)
            ]
            for c in range(5)
        ]
    low = sub < 7
    for n in (8, 4, 2, 1):
        on = (turn & n) != 0
        rolled = [[pltpu.roll(row[v], 7, 0) for v in range(n)] for row in x]
        out = []
        for c in range(5 if n > 1 else 4):
            row = []
            for v in range(16):
                if v + n < 16:
                    moved = x[c][v + n]
                else:
                    moved = jnp.where(low, rolled[c][v + n - 16], rolled[min(c + 1, 4)][v + n - 16])
                row.append(jnp.where(on, moved, x[c][v]))
            out.append(row)
        x = out
    return x


def index_kernel(owner_ref, cell_ref, weight_ref, key_ref, load_ref, start_ref, cells_ref):
    lane = lax.broadcasted_iota(I32, (8, 128), 1)
    sub = lax.broadcasted_iota(I32, (8, 128), 0)
    keys, loads = [], []
    for l in range(4):
        for j in range(4):
            rows = pl.ds(8 * j, 8)
            place = (8 * j + sub) * 128 + lane
            keys.append((owner_ref[l, rows, :] << 23) | (cell_ref[l, rows, :] << 12) | place)
            loads.append(weight_ref[l, rows, :])
    keys, loads = sort_links(keys, loads)
    start = owner_starts(keys)
    start_ref[...] = start
    for v in range(16):
        key_ref[pl.ds(8 * v, 8), :] = keys[v]
        load_ref[pl.ds(8 * v, 8), :] = loads[v]
    cells = [((k >> 12) & 2047).astype(F32) for k in keys]
    slots = owner_slots(cells, start)
    for c in range(4):
        cells_ref[c] = jnp.concatenate(slots[c], axis=0).T


def index_call(owner, cell, weight):
    vm = pl.BlockSpec(memory_space=pltpu.VMEM)
    return pl.pallas_call(
        index_kernel,
        out_shape=(
            jax.ShapeDtypeStruct((128, 128), I32),
            jax.ShapeDtypeStruct((128, 128), F32),
            jax.ShapeDtypeStruct((8, 128), I32),
            jax.ShapeDtypeStruct((4, 128, 128), F32),
        ),
        in_specs=[vm] * 3,
        out_specs=(vm,) * 4,
    )(owner, cell, weight)

BF16 = jnp.bfloat16


def link_values(surf_ref, key_ref, load_ref):
    keys = [key_ref[pl.ds(8 * v, 8), :] for v in range(16)]
    lanes = [k & 127 for k in keys]
    rows = [(k >> 7) & 31 for k in keys]
    found = [[jnp.zeros((8, 128), F32)] * 16 for _ in range(2)]
    for r in range(32):
        table = [jnp.broadcast_to(surf_ref[f, r : r + 1, :], (8, 128)) for f in range(2)]
        for v in range(16):
            here = rows[v] == r
            for f in range(2):
                found[f][v] = jnp.where(here, lanes_of(table[f], lanes[v]), found[f][v])
    loads = [load_ref[pl.ds(8 * v, 8), :] for v in range(16)]
    return [[loads[v] * found[f][v] for v in range(16)] for f in range(2)]


def write_sums(total, out_ref):
    for f in range(2):
        summed = total[32 * f : 32 * f + 16] + total[32 * f + 16 : 32 * f + 32]
        for h in range(16):
            out_ref[f : f + 1, 128 * h : 128 * h + 128] = summed[h : h + 1]


MESH = pl.DeviceIdType.MESH
mixing = 0.1


def at_lane(x, shift):
    return pltpu.roll(x, shift, 1)


def step_kernel(
    n_lat, n_lon,
    temp_hbm, salt_hbm, east_hbm, north_hbm, vdiff_hbm, kmt_ref,
    ft_ref, fs_ref, back_ref,
    tp, sp, vp, up, vd, inv, gain, c_mid, c_east, c_west, c_north, c_south,
    row_up, row_down, col_out, row_up2, row_down2, col_out2,
    g_north, g_south, g_west, g_east, g_north2, g_south2, g_west2, g_east2,
    edge, kp, load_sem, send_sem, recv_sem,
):
    lat, lon = lax.axis_index("lat"), lax.axis_index("lon")
    is_top = lat == n_lat - 1
    has_south = lat > 0
    north_id = (jnp.where(is_top, lat, lat + 1), jnp.where(is_top, n_lon - 1 - lon, lon))
    south_id = (jnp.maximum(lat - 1, 0), lon)
    east_id = (lat, lax.rem(lon + 1, n_lon))
    west_id = (lat, lax.rem(lon + n_lon - 1, n_lon))

    loads = [
        pltpu.make_async_copy(src, dst, load_sem.at[i])
        for i, (src, dst) in enumerate(
            (
                (temp_hbm, tp.at[:, 8:40, :]),
                (salt_hbm, sp.at[:, 8:40, :]),
                (east_hbm, up),
                (north_hbm, vp.at[:, 8:40, :]),
                (vdiff_hbm, vd),
            )
        )
    ]
    for load in loads:
        load.start()

    barrier = pltpu.get_barrier_semaphore()
    for peer in (north_id, east_id, west_id):
        pl.semaphore_signal(barrier, inc=1, device_id=peer, device_id_type=MESH)

    @pl.when(has_south)
    def _():
        pl.semaphore_signal(barrier, inc=1, device_id=south_id, device_id_type=MESH)

    @pl.when(jnp.logical_not(has_south))
    def _():
        g_south[...] = jnp.zeros_like(g_south)
        g_south2[...] = jnp.zeros_like(g_south2)

    lane = lax.broadcasted_iota(I32, (32, 128), 1)
    lane8 = lax.broadcasted_iota(I32, (8, 128), 1)
    kmt = kmt_ref[...].astype(F32)
    kp[8:40, :] = kmt

    def take_rows(src, row, dst, base):
        for g in range(8):
            dst[base + 8 * g : base + 8 * g + 8, :] = src[8 * g : 8 * g + 8, row, :]

    def put_rows(value, dst, g, row):
        dst[8 * g : 8 * g + 8, row, :] = value

    for load in loads[:4]:
        load.wait()
    for base, src in ((0, tp), (64, sp), (136, vp)):
        take_rows(src, 39, row_up, base)
    for base, src in ((0, tp), (64, sp)):
        take_rows(src, 8, row_down, base)
    row_up[128:136, :] = jnp.broadcast_to(kp[39:40, :], (8, 128))
    row_down[128:136, :] = jnp.broadcast_to(kp[8:9, :], (8, 128))

    def pack_level(k, packs):
        pair = (lane >> 1) == k
        fields = (tp[k, 8:40, :], sp[k, 8:40, :], up[k])
        return tuple(
            jnp.where(pair, at_lane(x, 2 * k + 1), p) for x, p in zip(fields, packs)
        )

    zero = jnp.zeros((32, 128), F32)
    packs = lax.fori_loop(0, 64, pack_level, (zero, zero, zero), unroll=4)
    col_out[0:32, :] = packs[0]
    col_out[32:64, :] = packs[1]
    col_out[64:96, :] = at_lane(kmt, 1)
    col_out[96:128, :] = packs[2]

    pl.semaphore_wait(barrier, jnp.where(has_south, 4, 3))

    def exchange(base, up_rows, top_rows, down_rows, east_rows, west_rows, bufs, ghosts):
        row_n, row_s, col = bufs
        north, south, west, east = ghosts

        def copy(src, dst, which, slot, peer):
            return pltpu.make_async_remote_copy(
                src_ref=src, dst_ref=dst, send_sem=send_sem.at[base + which],
                recv_sem=recv_sem.at[base + slot], device_id=peer, device_id_type=MESH,
            )

        to_north = copy(row_n.at[0:up_rows], south.at[0:up_rows], 0, 1, north_id)
        over_fold = copy(row_n.at[0:top_rows], north.at[0:top_rows], 0, 0, north_id)
        to_south = copy(row_s.at[0:down_rows], north.at[0:down_rows], 1, 0, south_id)
        to_east = copy(col.at[0:east_rows], west.at[0:east_rows], 2, 2, east_id)
        to_west = copy(col.at[0:west_rows], east.at[0:west_rows], 3, 3, west_id)

        def start():
            @pl.when(is_top)
            def _():
                over_fold.start()

            @pl.when(jnp.logical_not(is_top))
            def _():
                to_north.start()

            @pl.when(has_south)
            def _():
                to_south.start()

            to_east.start()
            to_west.start()

        def finish():
            @pl.when(is_top)
            def _():
                over_fold.wait_send()

            @pl.when(jnp.logical_not(is_top))
            def _():
                to_north.wait_send()

            @pl.when(has_south)
            def _():
                to_south.wait_send()
                to_north.wait_recv()

            to_south.wait_recv()
            to_east.wait()
            to_west.wait()

        return start, finish

    start, finish = exchange(
        0, 200, 136, 136, 128, 96, (row_up, row_down, col_out), (g_north, g_south, g_west, g_east)
    )
    start()

    loads[4].wait()

    def factor(k, carry):
        above, back = carry
        below = jnp.where((k + 1).astype(F32) < kmt, vd[k], 0.0)
        whole = 1.0 / (1.0 + below + above - above * back)
        inv[k] = whole
        gain[k] = above * whole
        back = below * whole
        back_ref[k] = back
        return below, back

    lax.fori_loop(0, 64, factor, (zero, zero), unroll=4)

    finish()

    mirror = jnp.where(is_top, 127 - lane8, lane8)

    def ghost_rows(north, south, fields):
        for base, dst in fields:
            for g in range(8):
                rows = slice(base + 8 * g, base + 8 * g + 8)
                put_rows(lanes_of(north[rows, :], mirror), dst, g, 40)
                put_rows(south[rows, :], dst, g, 7)

    def ghost_cols(west, east, count):
        for n in range(count):
            rows = slice(32 * n, 32 * n + 32)
            edge[rows, :] = jnp.where(
                (lane & 1) == 0, west[rows, :], at_lane(east[rows, :], 126)
            )

    ghost_rows(g_north, g_south, ((0, tp), (64, sp)))
    for g in range(8):
        put_rows(g_south[136 + 8 * g : 144 + 8 * g, :], vp, g, 7)
    kp[40:48, :] = lanes_of(g_north[128:136, :], mirror)
    kp[0:8, :] = g_south[128:136, :]
    ghost_cols(g_west, g_east, 3)
    edge[96:128, :] = g_west[96:128, :]

    first, last = lane == 0, lane == 127
    kmt_edge = edge[64:96, :]
    wet_east = jnp.minimum(kmt, jnp.where(last, kmt_edge, at_lane(kmt, 127)))
    wet_west = jnp.minimum(kmt, jnp.where(first, kmt_edge, at_lane(kmt, 1)))
    wet_north = jnp.minimum(kmt, kp[9:41, :])
    wet_south = jnp.minimum(kmt, kp[7:39, :])

    def stencil(src, row, k, turn, coefs):
        mid, east, west, north, south = coefs
        here = src[k, 8:40, :]
        ghost = at_lane(edge[row : row + 32, :], turn)
        on_east = jnp.where(last, ghost, at_lane(here, 127))
        on_west = jnp.where(first, ghost, at_lane(here, 1))
        return (
            mid * here + east * on_east + west * on_west
            + north * src[k, 9:41, :] + south * src[k, 7:39, :]
        )

    def down_first(k, carry):
        turn = lax.rem(128 - 2 * k, 128)
        level = k.astype(F32)
        whole = inv[k]
        half_e = 0.5 * up[k]
        half_w = jnp.where(first, 0.5 * at_lane(edge[96:128, :], turn), at_lane(half_e, 1))
        half_n = 0.5 * vp[k, 8:40, :]
        half_s = 0.5 * vp[k, 7:39, :]
        on_e, on_w = level < wet_east, level < wet_west
        on_n, on_s = level < wet_north, level < wet_south
        east = jnp.where(on_e, mixing - half_e, 0.0)
        west = jnp.where(on_w, mixing + half_w, 0.0)
        north = jnp.where(on_n, mixing - half_n, 0.0)
        south = jnp.where(on_s, mixing + half_s, 0.0)
        faces = (
            jnp.where(on_e, 2 * mixing, 0.0) + jnp.where(on_w, 2 * mixing, 0.0)
        ) + (jnp.where(on_n, 2 * mixing, 0.0) + jnp.where(on_s, 2 * mixing, 0.0))
        mid = (1.0 + (((east + west) + (north + south)) - faces)) * whole
        east, west, north, south = east * whole, west * whole, north * whole, south * whole
        c_mid[k], c_east[k], c_west[k], c_north[k], c_south[k] = mid, east, west, north, south
        coefs = (mid, east, west, north, south)
        above = gain[k]
        ft = stencil(tp, 0, k, turn, coefs) + above * carry[0]
        fs = stencil(sp, 32, k, turn, coefs) + above * carry[1]
        ft_ref[k] = ft
        fs_ref[k] = fs
        return ft, fs

    lax.fori_loop(0, 64, down_first, (zero, zero), unroll=2)

    def up_first(i, carry):
        xt, xs, pack_t, pack_s = carry
        k = 63 - i
        back = back_ref[k]
        xt = ft_ref[k] + back * xt
        xs = fs_ref[k] + back * xs
        tp[k, 8:40, :] = xt
        sp[k, 8:40, :] = xs
        pair = (lane >> 1) == k
        pack_t = jnp.where(pair, at_lane(xt, 2 * k + 1), pack_t)
        pack_s = jnp.where(pair, at_lane(xs, 2 * k + 1), pack_s)
        return xt, xs, pack_t, pack_s

    _, _, pack_t, pack_s = lax.fori_loop(0, 64, up_first, (zero, zero, zero, zero), unroll=4)
    col_out2[0:32, :] = pack_t
    col_out2[32:64, :] = pack_s
    for base, src in ((0, tp), (64, sp)):
        take_rows(src, 39, row_up2, base)
        take_rows(src, 8, row_down2, base)

    start, finish = exchange(
        4, 128, 128, 128, 64, 64,
        (row_up2, row_down2, col_out2), (g_north2, g_south2, g_west2, g_east2),
    )
    start()
    finish()
    ghost_rows(g_north2, g_south2, ((0, tp), (64, sp)))
    ghost_cols(g_west2, g_east2, 2)

    def down_second(k, carry):
        turn = lax.rem(128 - 2 * k, 128)
        coefs = (c_mid[k], c_east[k], c_west[k], c_north[k], c_south[k])
        above = gain[k]
        ft = stencil(tp, 0, k, turn, coefs) + above * carry[0]
        fs = stencil(sp, 32, k, turn, coefs) + above * carry[1]
        ft_ref[k] = ft
        fs_ref[k] = fs
        return ft, fs

    lax.fori_loop(0, 64, down_second, (zero, zero), unroll=2)


def step_call(n_lat, n_lon, temp, salt, east, north, vdiff, kmt):
    vm = pl.BlockSpec(memory_space=pltpu.VMEM)
    hbm = pl.BlockSpec(memory_space=pl.ANY)
    field = jax.ShapeDtypeStruct((64, 32, 128), F32)
    block, wide = pltpu.VMEM((64, 32, 128), F32), pltpu.VMEM((64, 48, 128), F32)
    rows = lambda n: pltpu.VMEM((n, 128), F32)
    return pl.pallas_call(
        functools.partial(step_kernel, n_lat, n_lon),
        out_shape=(field,) * 3,
        in_specs=[hbm] * 5 + [vm],
        out_specs=(vm,) * 3,
        scratch_shapes=[wide, wide, wide, block, block, block, block]
        + [block] * 5
        + [rows(n) for n in (200, 136, 128, 128, 128, 64)]
        + [rows(n) for n in (136, 200, 128, 96, 128, 128, 64, 64)]
        + [rows(128), rows(48)]
        + [pltpu.SemaphoreType.DMA((5,)), pltpu.SemaphoreType.DMA((8,)), pltpu.SemaphoreType.DMA((8,))],
        compiler_params=pltpu.CompilerParams(
            collective_id=1, has_side_effects=True, vmem_limit_bytes=48 << 20
        ),
    )(temp, salt, east, north, vdiff, kmt)


def back_kernel(ft_ref, fs_ref, back_ref, kmt_ref, t_ref, s_ref, surf_ref):
    def level(i, carry):
        k = 63 - i
        back = back_ref[k]
        xt = ft_ref[k] + back * carry[0]
        xs = fs_ref[k] + back * carry[1]
        t_ref[k] = xt
        s_ref[k] = xs
        return xt, xs

    zero = jnp.zeros((32, 128), F32)
    xt, xs = lax.fori_loop(0, 64, level, (zero, zero), unroll=4)
    wet = jnp.where(kmt_ref[...] > 0, 1.0, 0.0)
    surf_ref[0] = xt * wet
    surf_ref[1] = xs * wet


def back_call(ft, fs, back, kmt):
    vm = pl.BlockSpec(memory_space=pltpu.VMEM)
    field = jax.ShapeDtypeStruct((64, 32, 128), F32)
    return pl.pallas_call(
        back_kernel,
        out_shape=(field, field, jax.ShapeDtypeStruct((2, 32, 128), F32)),
        in_specs=[vm] * 4,
        out_specs=(vm,) * 3,
        compiler_params=pltpu.CompilerParams(vmem_limit_bytes=48 << 20),
    )(ft, fs, back, kmt)


GROUP = 16


def group_operands(recv_ref, first):
    high_id = lax.broadcasted_iota(I32, (16, 128), 0).astype(F32).astype(BF16)
    low_id = lax.broadcasted_iota(I32, (128, 128), 0).astype(F32).astype(BF16)
    left, right = [], []
    for q in range(GROUP):
        block = recv_ref[first + q]
        cell = block[8:12]
        high = jnp.floor(cell * (1.0 / 128.0))
        low = cell - 128.0 * high
        values = block[0:8]
        coarse = values.astype(BF16).astype(F32)
        fine = values - coarse
        for c in range(4):
            hits = jnp.broadcast_to(high[c : c + 1], (16, 128)).astype(BF16) == high_id
            part = []
            for f in range(2):
                for piece in (coarse, fine):
                    row = jnp.broadcast_to(piece[4 * f + c : 4 * f + c + 1], (16, 128)).astype(BF16)
                    part.append(jnp.where(hits, row, jnp.zeros_like(row)))
            left.append(jnp.concatenate(part, axis=0))
            match = jnp.broadcast_to(low[c : c + 1], (128, 128)).astype(BF16) == low_id
            right.append(jnp.where(match, jnp.ones((128, 128), BF16), jnp.zeros((128, 128), BF16)))
    return jnp.concatenate(left, axis=1), jnp.concatenate(right, axis=1)


def regrid_kernel(
    n_lat, n_lon, surf_ref, key_ref, load_ref, start_ref, cells_ref, out_ref,
    send, recv, ready, send_sem, recv_sem,
):
    n = n_lat * n_lon
    lat, lon = lax.axis_index("lat"), lax.axis_index("lon")
    me = lat * n_lon + lon
    barrier = pltpu.get_barrier_semaphore()

    def signal_lat(d, _):
        peer = (lax.rem(lat + d, n_lat), lon)
        pl.semaphore_signal(barrier, inc=1, device_id=peer, device_id_type=MESH)
        return 0

    def signal_lon(sem):
        def one(d, _):
            peer = (lat, lax.rem(lon + d, n_lon))
            pl.semaphore_signal(sem, inc=1, device_id=peer, device_id_type=MESH)
            return 0

        lax.fori_loop(1, n_lon, one, 0)

    lax.fori_loop(1, n_lat, signal_lat, 0)
    signal_lon(barrier)

    lane = lax.broadcasted_iota(I32, (8, 128), 1)
    sub = lax.broadcasted_iota(I32, (8, 128), 0)
    start = start_ref[...]
    after = jnp.where(lane < 127, pltpu.roll(start, 127, 1), 16384)
    count = after - start
    values = link_values(surf_ref, key_ref, load_ref)
    for c in range(4):
        send[:, 8 + c, :] = cells_ref[c]

    pl.semaphore_wait(barrier, n_lat + n_lon - 2)
    signal_lon(ready)

    for f in range(2):
        slots = owner_slots(values[f], start)
        for c in range(4):
            kept = [
                jnp.where(sub * 16 + (c * 128 + v) < count, slots[c][v], 0.0) for v in range(16)
            ]
            send[:, 4 * f + c, :] = jnp.concatenate(kept, axis=0).T

    pl.semaphore_wait(ready, n_lon - 1)

    def send_one(d, _):
        to = lax.rem(me + d, n)
        pltpu.make_async_remote_copy(
            src_ref=send.at[to], dst_ref=recv.at[d], send_sem=send_sem,
            recv_sem=recv_sem.at[d // GROUP],
            device_id=(to // n_lon, lax.rem(to, n_lon)), device_id_type=MESH,
        ).start()
        return 0

    lax.fori_loop(1, n, send_one, 0)
    recv[0] = send[me]

    def arrived(lo, hi, g):
        part = recv.at[lo:hi] if isinstance(lo, int) else recv.at[pl.ds(lo, hi)]
        pltpu.make_async_copy(part, part, recv_sem.at[g]).wait()

    def add_group(g, total):
        @pl.when(g == 0)
        def _():
            arrived(1, GROUP, 0)

        @pl.when(g > 0)
        def _():
            arrived(pl.multiple_of(g * GROUP, GROUP), GROUP, g)

        left, right = group_operands(recv, g * GROUP)
        return total + lax.dot_general(
            right, left, (((1,), (1,)), ((), ())), preferred_element_type=F32
        )

    total = lax.fori_loop(0, n // GROUP, add_group, jnp.zeros((128, 64), F32))
    write_sums(total.T, out_ref)
    sent = send.at[0 : n - 1]
    pltpu.make_async_copy(sent, sent, send_sem).wait()


def regrid_call(n_lat, n_lon, surf, key, load, start, cells):
    vm = pl.BlockSpec(memory_space=pltpu.VMEM)
    n = n_lat * n_lon
    return pl.pallas_call(
        functools.partial(regrid_kernel, n_lat, n_lon),
        out_shape=jax.ShapeDtypeStruct((2, 2048), F32),
        in_specs=[vm] * 5,
        out_specs=vm,
        scratch_shapes=[
            pltpu.VMEM((128, 12, 128), F32),
            pltpu.VMEM((128, 12, 128), F32),
            pltpu.SemaphoreType.REGULAR,
            pltpu.SemaphoreType.DMA,
            pltpu.SemaphoreType.DMA((n // GROUP,)),
        ],
        compiler_params=pltpu.CompilerParams(
            collective_id=2, has_side_effects=True, vmem_limit_bytes=32 << 20
        ),
    )(surf, key, load, start, cells)


def solution(mesh):
    n_lat, n_lon = mesh.shape["lat"], mesh.shape["lon"]

    def body(temp, salt, u_east, v_north, vdiff, kmt, owner, atmo_cell, weight):
        key, load, start, cells = index_call(owner, atmo_cell, weight)
        ft, fs, back = step_call(n_lat, n_lon, temp, salt, u_east, v_north, vdiff, kmt)
        t_out, s_out, surf = back_call(ft, fs, back, kmt)
        atmo = regrid_call(n_lat, n_lon, surf, key, load, start, cells)
        return t_out, s_out, atmo

    level, flat = P(None, "lat", "lon"), P("lat", "lon")
    return jax.shard_map(
        body,
        mesh=mesh,
        in_specs=(level,) * 5 + (flat,) + (level,) * 3,
        out_specs=(level, level, P(None, ("lat", "lon"))),
        check_vma=False,
    )
```

```python
import functools

import jax
import jax.numpy as jnp
from jax import lax
from jax.experimental import pallas as pl
from jax.experimental.pallas import tpu as pltpu
from jax.sharding import PartitionSpec as P

I32 = jnp.int32
F32 = jnp.float32
BF16 = jnp.bfloat16
MESH = pl.DeviceIdType.MESH
mixing = 0.1
GROUP = 16
FIRST_MERGES = 12
VMEM_MB = 60
HAND_MB = 60


def lanes_of(x, idx):
    return jnp.take_along_axis(x, idx, axis=1, mode="promise_in_bounds")


def owner_starts(keys):
    lane = lax.broadcasted_iota(I32, (8, 128), 1)
    first = jnp.broadcast_to(keys[0][0:1, :], (8, 128))
    bound = lane << 23
    count = jnp.zeros((8, 128), I32)
    for step in (128, 64, 32, 16, 8, 4, 2, 1):
        trial = count + step
        value = lanes_of(first, jnp.minimum(trial - 1, 127))
        fits = jnp.logical_and(trial <= 128, value < bound)
        count = jnp.where(fits, trial, count)
    column = jnp.maximum(count - 1, 0)
    within = jnp.zeros((8, 128), I32)
    for v in range(16):
        within = within + jnp.where(lanes_of(keys[v], column) < bound, 1, 0)
    within = jnp.broadcast_to(jnp.sum(within, axis=0, keepdims=True), (8, 128))
    return jnp.where(count > 0, column * 128 + within, 0)


def owner_slots(tiles, start):
    sub = lax.broadcasted_iota(I32, (8, 128), 0)
    column = start >> 7
    turn = start & 127
    x = []
    for c in range(5):
        idx = jnp.minimum(column + c, 127)
        x.append([lanes_of(tiles[v], idx) for v in range(16)])
    for n in (64, 32, 16):
        on = (turn & n) != 0
        a = n // 16
        low = sub < 8 - a
        rolled = [[pltpu.roll(t, 8 - a, 0) for t in row] for row in x]
        x = [
            [
                jnp.where(on, jnp.where(low, rolled[c][v], rolled[min(c + 1, 4)][v]), x[c][v])
                for v in range(16)
            ]
            for c in range(5)
        ]
    low = sub < 7
    for n in (8, 4, 2, 1):
        on = (turn & n) != 0
        rolled = [[pltpu.roll(row[v], 7, 0) for v in range(n)] for row in x]
        out = []
        for c in range(5 if n > 1 else 4):
            row = []
            for v in range(16):
                if v + n < 16:
                    moved = x[c][v + n]
                else:
                    moved = jnp.where(low, rolled[c][v + n - 16], rolled[min(c + 1, 4)][v + n - 16])
                row.append(jnp.where(on, moved, x[c][v]))
            out.append(row)
        x = out
    return x


def link_values(surf_ref, key_ref, load_ref):
    keys = [key_ref[pl.ds(8 * v, 8), :] for v in range(16)]
    lanes = [k & 127 for k in keys]
    rows = [(k >> 7) & 31 for k in keys]
    found = [[jnp.zeros((8, 128), F32)] * 16 for _ in range(2)]
    for r in range(32):
        table = [jnp.broadcast_to(surf_ref[f, r : r + 1, :], (8, 128)) for f in range(2)]
        for v in range(16):
            here = rows[v] == r
            for f in range(2):
                found[f][v] = jnp.where(here, lanes_of(table[f], lanes[v]), found[f][v])
    loads = [load_ref[pl.ds(8 * v, 8), :] for v in range(16)]
    return [[loads[v] * found[f][v] for v in range(16)] for f in range(2)]


def write_sums(total, out_ref):
    for f in range(2):
        summed = total[32 * f : 32 * f + 16] + total[32 * f + 16 : 32 * f + 32]
        for h in range(16):
            out_ref[f : f + 1, 128 * h : 128 * h + 128] = summed[h : h + 1]


def at_lane(x, shift):
    return pltpu.roll(x, shift, 1)


def group_operands(recv_ref, first):
    high_id = lax.broadcasted_iota(I32, (16, 128), 0).astype(F32).astype(BF16)
    low_id = lax.broadcasted_iota(I32, (128, 128), 0).astype(F32).astype(BF16)
    left, right = [], []
    for q in range(GROUP):
        block = recv_ref[first + q]
        cell = block[8:12]
        high = jnp.floor(cell * (1.0 / 128.0))
        low = cell - 128.0 * high
        values = block[0:8]
        coarse = values.astype(BF16).astype(F32)
        fine = values - coarse
        for c in range(4):
            hits = jnp.broadcast_to(high[c : c + 1], (16, 128)).astype(BF16) == high_id
            part = []
            for f in range(2):
                for piece in (coarse, fine):
                    row = jnp.broadcast_to(piece[4 * f + c : 4 * f + c + 1], (16, 128)).astype(BF16)
                    part.append(jnp.where(hits, row, jnp.zeros_like(row)))
            left.append(jnp.concatenate(part, axis=0))
            match = jnp.broadcast_to(low[c : c + 1], (128, 128)).astype(BF16) == low_id
            right.append(jnp.where(match, jnp.ones((128, 128), BF16), jnp.zeros((128, 128), BF16)))
    return jnp.concatenate(left, axis=1), jnp.concatenate(right, axis=1)


def merges(keys, loads, tops):
    lane = lax.broadcasted_iota(I32, (8, 128), 1)
    sub = lax.broadcasted_iota(I32, (8, 128), 0)

    def bit(b):
        if b < 4 or b >= 14:
            return None
        where = sub >> (b - 4) if b < 7 else lane >> (b - 7)
        return (where & 1) == 1

    for top in tops:
        for b in range(top - 1, -1, -1):
            down = bit(top)
            new_k, new_w = list(keys), list(loads)
            if b < 4:
                for v in range(16):
                    if (v >> b) & 1:
                        continue
                    u = v | (1 << b)
                    if top < 4 and (v >> top) & 1:
                        swap = keys[v] < keys[u]
                    else:
                        swap = keys[v] > keys[u]
                    if down is not None:
                        swap = jnp.logical_xor(swap, down)
                    new_k[v] = jnp.where(swap, keys[u], keys[v])
                    new_k[u] = jnp.where(swap, keys[v], keys[u])
                    new_w[v] = jnp.where(swap, loads[u], loads[v])
                    new_w[u] = jnp.where(swap, loads[v], loads[u])
            else:
                keep_max = bit(b) if down is None else jnp.logical_xor(bit(b), down)
                if b < 7:
                    idx, axis = sub ^ (1 << (b - 4)), 0
                else:
                    idx, axis = lane ^ (1 << (b - 7)), 1
                for v in range(16):
                    k, w = keys[v], loads[v]
                    pk = jnp.take_along_axis(k, idx, axis=axis, mode="promise_in_bounds")
                    pw = jnp.take_along_axis(w, idx, axis=axis, mode="promise_in_bounds")
                    take = jnp.logical_or(
                        jnp.logical_and(keep_max, pk > k),
                        jnp.logical_and(jnp.logical_not(keep_max), pk < k),
                    )
                    new_k[v] = jnp.where(take, pk, k)
                    new_w[v] = jnp.where(take, pw, w)
            keys, loads = new_k, new_w
    return keys, loads


def whole_kernel(
    n_lat, n_lon,
    temp_hbm, salt_hbm, east_hbm, north_hbm, vdiff_hbm, kmt_ref, owner_hbm, cell_hbm, weight_hbm,
    t_hbm, s_hbm, atmo_ref,
    t_ref, s_ref, tp, sp, vp, up, vd, inv, gain, back_ref, c_mid, c_east, c_west, c_north, c_south,
    row_up, row_down, col_out, row_up2, row_down2, col_out2,
    g_north, g_south, g_west, g_east, g_north2, g_south2, g_west2, g_east2,
    edge, kp, owner_ref, cell_ref, weight_ref, key_ref, load_ref, surf_ref, send, recv,
    load_sem, store_sem, send_sem, recv_sem, ready, all_send, all_recv,
):
    n = n_lat * n_lon
    lat, lon = lax.axis_index("lat"), lax.axis_index("lon")
    me = lat * n_lon + lon
    is_top = lat == n_lat - 1
    has_south = lat > 0
    north_id = (jnp.where(is_top, lat, lat + 1), jnp.where(is_top, n_lon - 1 - lon, lon))
    south_id = (jnp.maximum(lat - 1, 0), lon)
    east_id = (lat, lax.rem(lon + 1, n_lon))
    west_id = (lat, lax.rem(lon + n_lon - 1, n_lon))

    loads = [
        pltpu.make_async_copy(src, dst, load_sem.at[i])
        for i, (src, dst) in enumerate(
            (
                (temp_hbm, tp.at[:, 8:40, :]),
                (salt_hbm, sp.at[:, 8:40, :]),
                (east_hbm, up),
                (north_hbm, vp.at[:, 8:40, :]),
                (vdiff_hbm, vd),
                (owner_hbm, owner_ref),
                (cell_hbm, cell_ref),
                (weight_hbm, weight_ref),
            )
        )
    ]
    for load in loads:
        load.start()

    barrier = pltpu.get_barrier_semaphore()

    def greet_row(sem):
        def one(d, _):
            peer = (lat, lax.rem(lon + d, n_lon))
            pl.semaphore_signal(sem, inc=1, device_id=peer, device_id_type=MESH)
            return 0

        lax.fori_loop(1, n_lon, one, 0)

    def greet_column(d, _):
        peer = (lax.rem(lat + d, n_lat), lon)
        pl.semaphore_signal(barrier, inc=1, device_id=peer, device_id_type=MESH)
        return 0

    lax.fori_loop(1, n_lat, greet_column, 0)
    greet_row(barrier)

    @pl.when(jnp.logical_not(has_south))
    def _():
        g_south[...] = jnp.zeros_like(g_south)
        g_south2[...] = jnp.zeros_like(g_south2)

    lane = lax.broadcasted_iota(I32, (32, 128), 1)
    lane8 = lax.broadcasted_iota(I32, (8, 128), 1)
    sub8 = lax.broadcasted_iota(I32, (8, 128), 0)
    kmt = kmt_ref[...].astype(F32)
    kp[8:40, :] = kmt

    def take_rows(src, row, dst, base):
        for g in range(8):
            dst[base + 8 * g : base + 8 * g + 8, :] = src[8 * g : 8 * g + 8, row, :]

    def put_rows(value, dst, g, row):
        dst[8 * g : 8 * g + 8, row, :] = value

    for load in loads[:4]:
        load.wait()
    for base, src in ((0, tp), (64, sp), (136, vp)):
        take_rows(src, 39, row_up, base)
    for base, src in ((0, tp), (64, sp)):
        take_rows(src, 8, row_down, base)
    row_up[128:136, :] = jnp.broadcast_to(kp[39:40, :], (8, 128))
    row_down[128:136, :] = jnp.broadcast_to(kp[8:9, :], (8, 128))

    def pack_level(k, packs):
        pair = (lane >> 1) == k
        fields = (tp[k, 8:40, :], sp[k, 8:40, :], up[k])
        return tuple(
            jnp.where(pair, at_lane(x, 2 * k + 1), p) for x, p in zip(fields, packs)
        )

    zero = jnp.zeros((32, 128), F32)
    packs = lax.fori_loop(0, 64, pack_level, (zero, zero, zero), unroll=4)
    col_out[0:32, :] = packs[0]
    col_out[32:64, :] = packs[1]
    col_out[64:96, :] = at_lane(kmt, 1)
    col_out[96:128, :] = packs[2]

    pl.semaphore_wait(barrier, n_lat + n_lon - 2)

    def exchange(base, up_rows, top_rows, down_rows, east_rows, west_rows, bufs, ghosts):
        row_n, row_s, col = bufs
        north, south, west, east = ghosts

        def copy(src, dst, which, slot, peer):
            return pltpu.make_async_remote_copy(
                src_ref=src, dst_ref=dst, send_sem=send_sem.at[base + which],
                recv_sem=recv_sem.at[base + slot], device_id=peer, device_id_type=MESH,
            )

        to_north = copy(row_n.at[0:up_rows], south.at[0:up_rows], 0, 1, north_id)
        over_fold = copy(row_n.at[0:top_rows], north.at[0:top_rows], 0, 0, north_id)
        to_south = copy(row_s.at[0:down_rows], north.at[0:down_rows], 1, 0, south_id)
        to_east = copy(col.at[0:east_rows], west.at[0:east_rows], 2, 2, east_id)
        to_west = copy(col.at[0:west_rows], east.at[0:west_rows], 3, 3, west_id)

        def start():
            @pl.when(is_top)
            def _():
                over_fold.start()

            @pl.when(jnp.logical_not(is_top))
            def _():
                to_north.start()

            @pl.when(has_south)
            def _():
                to_south.start()

            to_east.start()
            to_west.start()

        def finish():
            @pl.when(is_top)
            def _():
                over_fold.wait_send()

            @pl.when(jnp.logical_not(is_top))
            def _():
                to_north.wait_send()

            @pl.when(has_south)
            def _():
                to_south.wait_send()
                to_north.wait_recv()

            to_south.wait_recv()
            to_east.wait()
            to_west.wait()

        return start, finish

    start, finish = exchange(
        0, 200, 136, 136, 128, 96, (row_up, row_down, col_out), (g_north, g_south, g_west, g_east)
    )
    start()
    greet_row(ready)

    loads[4].wait()

    def factor(k, carry):
        above, back = carry
        below = jnp.where((k + 1).astype(F32) < kmt, vd[k], 0.0)
        whole = 1.0 / (1.0 + below + above - above * back)
        inv[k] = whole
        gain[k] = above * whole
        back = below * whole
        back_ref[k] = back
        return below, back

    lax.fori_loop(0, 64, factor, (zero, zero), unroll=4)

    for load in loads[5:]:
        load.wait()

    def hold(keys, loads):
        for v in range(16):
            key_ref[8 * v : 8 * v + 8, :] = keys[v]
            load_ref[8 * v : 8 * v + 8, :] = loads[v]

    def held(ref):
        return [ref[8 * v : 8 * v + 8, :] for v in range(16)]

    keys, shares = [], []
    for l in range(4):
        for j in range(4):
            rows = slice(8 * j, 8 * j + 8)
            place = (8 * j + sub8) * 128 + lane8
            keys.append((owner_ref[l, rows, :] << 23) | (cell_ref[l, rows, :] << 12) | place)
            shares.append(weight_ref[l, rows, :])
    hold(*merges(keys, shares, range(1, FIRST_MERGES + 1)))

    finish()

    mirror = jnp.where(is_top, 127 - lane8, lane8)

    def ghost_rows(north, south, fields):
        for base, dst in fields:
            for g in range(8):
                rows = slice(base + 8 * g, base + 8 * g + 8)
                put_rows(lanes_of(north[rows, :], mirror), dst, g, 40)
                put_rows(south[rows, :], dst, g, 7)

    def ghost_cols(west, east, count):
        for i in range(count):
            rows = slice(32 * i, 32 * i + 32)
            edge[rows, :] = jnp.where(
                (lane & 1) == 0, west[rows, :], at_lane(east[rows, :], 126)
            )

    ghost_rows(g_north, g_south, ((0, tp), (64, sp)))
    for g in range(8):
        put_rows(g_south[136 + 8 * g : 144 + 8 * g, :], vp, g, 7)
    kp[40:48, :] = lanes_of(g_north[128:136, :], mirror)
    kp[0:8, :] = g_south[128:136, :]
    ghost_cols(g_west, g_east, 3)
    edge[96:128, :] = g_west[96:128, :]

    first, last = lane == 0, lane == 127
    kmt_edge = edge[64:96, :]
    wet_east = jnp.minimum(kmt, jnp.where(last, kmt_edge, at_lane(kmt, 127)))
    wet_west = jnp.minimum(kmt, jnp.where(first, kmt_edge, at_lane(kmt, 1)))
    wet_north = jnp.minimum(kmt, kp[9:41, :])
    wet_south = jnp.minimum(kmt, kp[7:39, :])

    def stencil(src, row, k, turn, coefs):
        mid, east, west, north, south = coefs
        here = src[k, 8:40, :]
        ghost = at_lane(edge[row : row + 32, :], turn)
        on_east = jnp.where(last, ghost, at_lane(here, 127))
        on_west = jnp.where(first, ghost, at_lane(here, 1))
        return (
            mid * here + east * on_east + west * on_west
            + north * src[k, 9:41, :] + south * src[k, 7:39, :]
        )

    def advance(k, carry, turn, coefs):
        above = gain[k]
        ft = stencil(tp, 0, k, turn, coefs) + above * carry[0]
        fs = stencil(sp, 32, k, turn, coefs) + above * carry[1]
        t_ref[k] = ft
        s_ref[k] = fs
        return ft, fs

    def down_first(k, carry):
        turn = lax.rem(128 - 2 * k, 128)
        level = k.astype(F32)
        whole = inv[k]
        half_e = 0.5 * up[k]
        half_w = jnp.where(first, 0.5 * at_lane(edge[96:128, :], turn), at_lane(half_e, 1))
        half_n = 0.5 * vp[k, 8:40, :]
        half_s = 0.5 * vp[k, 7:39, :]
        on_e, on_w = level < wet_east, level < wet_west
        on_n, on_s = level < wet_north, level < wet_south
        east = jnp.where(on_e, mixing - half_e, 0.0)
        west = jnp.where(on_w, mixing + half_w, 0.0)
        north = jnp.where(on_n, mixing - half_n, 0.0)
        south = jnp.where(on_s, mixing + half_s, 0.0)
        faces = (
            jnp.where(on_e, 2 * mixing, 0.0) + jnp.where(on_w, 2 * mixing, 0.0)
        ) + (jnp.where(on_n, 2 * mixing, 0.0) + jnp.where(on_s, 2 * mixing, 0.0))
        mid = (1.0 + (((east + west) + (north + south)) - faces)) * whole
        east, west, north, south = east * whole, west * whole, north * whole, south * whole
        c_mid[k], c_east[k], c_west[k], c_north[k], c_south[k] = mid, east, west, north, south
        return advance(k, carry, turn, (mid, east, west, north, south))

    lax.fori_loop(0, 64, down_first, (zero, zero), unroll=2)

    def up_first(i, carry):
        xt, xs, pack_t, pack_s = carry
        k = 63 - i
        back = back_ref[k]
        xt = t_ref[k] + back * xt
        xs = s_ref[k] + back * xs
        tp[k, 8:40, :] = xt
        sp[k, 8:40, :] = xs
        pair = (lane >> 1) == k
        pack_t = jnp.where(pair, at_lane(xt, 2 * k + 1), pack_t)
        pack_s = jnp.where(pair, at_lane(xs, 2 * k + 1), pack_s)
        return xt, xs, pack_t, pack_s

    _, _, pack_t, pack_s = lax.fori_loop(0, 64, up_first, (zero, zero, zero, zero), unroll=4)
    col_out2[0:32, :] = pack_t
    col_out2[32:64, :] = pack_s
    for base, src in ((0, tp), (64, sp)):
        take_rows(src, 39, row_up2, base)
        take_rows(src, 8, row_down2, base)

    start, finish = exchange(
        4, 128, 128, 128, 64, 64,
        (row_up2, row_down2, col_out2), (g_north2, g_south2, g_west2, g_east2),
    )
    start()

    keys, shares = merges(held(key_ref), held(load_ref), range(FIRST_MERGES + 1, 15))
    hold(keys, shares)
    begin = owner_starts(keys)
    cells = owner_slots([((k >> 12) & 2047).astype(F32) for k in keys], begin)
    for c in range(4):
        send[:, 8 + c, :] = jnp.concatenate(cells[c], axis=0).T

    finish()
    ghost_rows(g_north2, g_south2, ((0, tp), (64, sp)))
    ghost_cols(g_west2, g_east2, 2)

    def down_second(k, carry):
        turn = lax.rem(128 - 2 * k, 128)
        return advance(k, carry, turn, (c_mid[k], c_east[k], c_west[k], c_north[k], c_south[k]))

    lax.fori_loop(0, 64, down_second, (zero, zero), unroll=2)

    def up_second(i, carry):
        k = 63 - i
        back = back_ref[k]
        xt = t_ref[k] + back * carry[0]
        xs = s_ref[k] + back * carry[1]
        t_ref[k] = xt
        s_ref[k] = xs
        return xt, xs

    xt, xs = lax.fori_loop(0, 64, up_second, (zero, zero), unroll=4)
    stores = [
        pltpu.make_async_copy(t_ref, t_hbm, store_sem.at[0]),
        pltpu.make_async_copy(s_ref, s_hbm, store_sem.at[1]),
    ]
    for store in stores:
        store.start()
    wet = jnp.where(kmt > 0.0, 1.0, 0.0)
    surf_ref[0] = xt * wet
    surf_ref[1] = xs * wet

    values = link_values(surf_ref, key_ref, load_ref)
    count = jnp.where(lane8 < 127, pltpu.roll(begin, 127, 1), 16384) - begin
    for f in range(2):
        slots = owner_slots(values[f], begin)
        for c in range(4):
            kept = [
                jnp.where(sub8 * 16 + (c * 128 + v) < count, slots[c][v], 0.0) for v in range(16)
            ]
            send[:, 4 * f + c, :] = jnp.concatenate(kept, axis=0).T

    pl.semaphore_wait(ready, n_lon - 1)

    def send_one(d, _):
        to = lax.rem(me + d, n)
        pltpu.make_async_remote_copy(
            src_ref=send.at[to], dst_ref=recv.at[d], send_sem=all_send,
            recv_sem=all_recv.at[d // GROUP],
            device_id=(to // n_lon, lax.rem(to, n_lon)), device_id_type=MESH,
        ).start()
        return 0

    lax.fori_loop(1, n, send_one, 0)
    recv[0] = send[me]

    def add_group(g, total):
        @pl.when(g == 0)
        def _():
            part = recv.at[1:GROUP]
            pltpu.make_async_copy(part, part, all_recv.at[0]).wait()

        @pl.when(g > 0)
        def _():
            part = recv.at[pl.ds(pl.multiple_of(g * GROUP, GROUP), GROUP)]
            pltpu.make_async_copy(part, part, all_recv.at[g]).wait()

        left, right = group_operands(recv, g * GROUP)
        return total + lax.dot_general(
            right, left, (((1,), (1,)), ((), ())), preferred_element_type=F32
        )

    total = lax.fori_loop(0, n // GROUP, add_group, jnp.zeros((128, 64), F32))
    write_sums(total.T, atmo_ref)
    for store in stores:
        store.wait()
    sent = send.at[0 : n - 1]
    pltpu.make_async_copy(sent, sent, all_send).wait()


def whole_call(n_lat, n_lon, temp, salt, east, north, vdiff, kmt, owner, cell, weight):
    vm = pl.BlockSpec(memory_space=pltpu.VMEM)
    hbm = pl.BlockSpec(memory_space=pltpu.HBM)
    field = jax.ShapeDtypeStruct((64, 32, 128), F32)
    block, wide = pltpu.VMEM((64, 32, 128), F32), pltpu.VMEM((64, 48, 128), F32)
    links = pltpu.VMEM((4, 32, 128), I32)
    dma = pltpu.SemaphoreType.DMA
    n = n_lat * n_lon

    def rows(count, dtype=F32):
        return pltpu.VMEM((count, 128), dtype)

    return pl.pallas_call(
        functools.partial(whole_kernel, n_lat, n_lon),
        out_shape=(field, field, jax.ShapeDtypeStruct((2, 2048), F32)),
        in_specs=[hbm] * 5 + [vm] + [hbm] * 3,
        out_specs=(hbm, hbm, vm),
        scratch_shapes=[block] * 2
        + [wide] * 3
        + [block] * 10
        + [rows(r) for r in (200, 136, 128, 128, 128, 64)]
        + [rows(r) for r in (136, 200, 128, 96, 128, 128, 64, 64)]
        + [rows(128), rows(48), links, links, pltpu.VMEM((4, 32, 128), F32)]
        + [rows(128, I32), rows(128), pltpu.VMEM((2, 32, 128), F32)]
        + [pltpu.VMEM((128, 12, 128), F32)] * 2
        + [dma((8,)), dma((2,)), dma((8,)), dma((8,)), pltpu.SemaphoreType.REGULAR, dma, dma((n // GROUP,))],
        compiler_params=pltpu.CompilerParams(
            collective_id=1, has_side_effects=True, vmem_limit_bytes=VMEM_MB << 20
        ),
    )(temp, salt, east, north, vdiff, kmt, owner, cell, weight)


def hand_kernel(t_in, s_in, atmo_in, t_out, s_out, atmo_out, t_ref, s_ref, atmo_ref, in_sem, out_sem):
    parts = [(atmo_in, atmo_ref, atmo_out)]
    for src, mid, dst in ((t_in, t_ref, t_out), (s_in, s_ref, s_out)):
        for i in range(4):
            rows = slice(16 * i, 16 * i + 16)
            parts.append((src.at[rows], mid.at[rows], dst.at[rows]))
    gets = [pltpu.make_async_copy(p[0], p[1], in_sem.at[i]) for i, p in enumerate(parts)]
    puts = [pltpu.make_async_copy(p[1], p[2], out_sem.at[i]) for i, p in enumerate(parts)]
    for get in gets:
        get.start()
    for get, put in zip(gets, puts):
        get.wait()
        put.start()
    for put in puts:
        put.wait()


def hand_call(temp, salt, atmo):
    hbm = pl.BlockSpec(memory_space=pl.ANY)
    shapes = [jax.ShapeDtypeStruct(a.shape, a.dtype) for a in (temp, salt, atmo)]
    return pl.pallas_call(
        hand_kernel,
        out_shape=tuple(shapes),
        in_specs=[hbm] * 3,
        out_specs=(hbm,) * 3,
        scratch_shapes=[pltpu.VMEM(a.shape, a.dtype) for a in shapes]
        + [pltpu.SemaphoreType.DMA((9,))] * 2,
        compiler_params=pltpu.CompilerParams(vmem_limit_bytes=HAND_MB << 20),
    )(temp, salt, atmo)


def solution(mesh):
    n_lat, n_lon = mesh.shape["lat"], mesh.shape["lon"]
    level, flat = P(None, "lat", "lon"), P("lat", "lon")
    return jax.shard_map(
        lambda *a: hand_call(*whole_call(n_lat, n_lon, *a)),
        mesh=mesh,
        in_specs=(level,) * 5 + (flat,) + (level,) * 3,
        out_specs=(level, level, P(None, ("lat", "lon"))),
        check_vma=False,
    )
```

```python
import functools

import jax
import jax.numpy as jnp
from jax import lax
from jax.experimental import pallas as pl
from jax.experimental.pallas import tpu as pltpu
from jax.sharding import PartitionSpec as P

I32 = jnp.int32
F32 = jnp.float32
BF16 = jnp.bfloat16
MESH = pl.DeviceIdType.MESH
mixing = 0.1
GROUP = 16
FIRST_MERGES = 12
VMEM_MB = 32
HAND_MB = 8


def lanes_of(x, idx):
    return jnp.take_along_axis(x, idx, axis=1, mode="promise_in_bounds")


def owner_starts(keys):
    lane = lax.broadcasted_iota(I32, (8, 128), 1)
    first = jnp.broadcast_to(keys[0][0:1, :], (8, 128))
    bound = lane << 23
    count = jnp.zeros((8, 128), I32)
    for step in (128, 64, 32, 16, 8, 4, 2, 1):
        trial = count + step
        value = lanes_of(first, jnp.minimum(trial - 1, 127))
        fits = jnp.logical_and(trial <= 128, value < bound)
        count = jnp.where(fits, trial, count)
    column = jnp.maximum(count - 1, 0)
    within = jnp.zeros((8, 128), I32)
    for v in range(16):
        within = within + jnp.where(lanes_of(keys[v], column) < bound, 1, 0)
    within = jnp.broadcast_to(jnp.sum(within, axis=0, keepdims=True), (8, 128))
    return jnp.where(count > 0, column * 128 + within, 0)


def owner_slots(tiles, start):
    sub = lax.broadcasted_iota(I32, (8, 128), 0)
    column = start >> 7
    turn = start & 127
    x = []
    for c in range(5):
        idx = jnp.minimum(column + c, 127)
        x.append([lanes_of(tiles[v], idx) for v in range(16)])
    for n in (64, 32, 16):
        on = (turn & n) != 0
        a = n // 16
        low = sub < 8 - a
        rolled = [[pltpu.roll(t, 8 - a, 0) for t in row] for row in x]
        x = [
            [
                jnp.where(on, jnp.where(low, rolled[c][v], rolled[min(c + 1, 4)][v]), x[c][v])
                for v in range(16)
            ]
            for c in range(5)
        ]
    low = sub < 7
    for n in (8, 4, 2, 1):
        on = (turn & n) != 0
        rolled = [[pltpu.roll(row[v], 7, 0) for v in range(n)] for row in x]
        out = []
        for c in range(5 if n > 1 else 4):
            row = []
            for v in range(16):
                if v + n < 16:
                    moved = x[c][v + n]
                else:
                    moved = jnp.where(low, rolled[c][v + n - 16], rolled[min(c + 1, 4)][v + n - 16])
                row.append(jnp.where(on, moved, x[c][v]))
            out.append(row)
        x = out
    return x


def link_values(surf_ref, key_ref, load_ref):
    keys = [key_ref[pl.ds(8 * v, 8), :] for v in range(16)]
    lanes = [k & 127 for k in keys]
    rows = [(k >> 7) & 31 for k in keys]
    found = [[jnp.zeros((8, 128), F32)] * 16 for _ in range(2)]
    for r in range(32):
        table = [jnp.broadcast_to(surf_ref[f, r : r + 1, :], (8, 128)) for f in range(2)]
        for v in range(16):
            here = rows[v] == r
            for f in range(2):
                found[f][v] = jnp.where(here, lanes_of(table[f], lanes[v]), found[f][v])
    loads = [load_ref[pl.ds(8 * v, 8), :] for v in range(16)]
    return [[loads[v] * found[f][v] for v in range(16)] for f in range(2)]


def write_sums(total, out_ref):
    for f in range(2):
        summed = total[32 * f : 32 * f + 16] + total[32 * f + 16 : 32 * f + 32]
        for h in range(16):
            out_ref[f : f + 1, 128 * h : 128 * h + 128] = summed[h : h + 1]


def at_lane(x, shift):
    return pltpu.roll(x, shift, 1)


def group_operands(recv_ref, first):
    high_id = lax.broadcasted_iota(I32, (16, 128), 0).astype(F32).astype(BF16)
    low_id = lax.broadcasted_iota(I32, (128, 128), 0).astype(F32).astype(BF16)
    left, right = [], []
    for q in range(GROUP):
        block = recv_ref[first + q]
        cell = block[8:12]
        high = jnp.floor(cell * (1.0 / 128.0))
        low = cell - 128.0 * high
        values = block[0:8]
        coarse = values.astype(BF16).astype(F32)
        fine = values - coarse
        for c in range(4):
            hits = jnp.broadcast_to(high[c : c + 1], (16, 128)).astype(BF16) == high_id
            part = []
            for f in range(2):
                for piece in (coarse, fine):
                    row = jnp.broadcast_to(piece[4 * f + c : 4 * f + c + 1], (16, 128)).astype(BF16)
                    part.append(jnp.where(hits, row, jnp.zeros_like(row)))
            left.append(jnp.concatenate(part, axis=0))
            match = jnp.broadcast_to(low[c : c + 1], (128, 128)).astype(BF16) == low_id
            right.append(jnp.where(match, jnp.ones((128, 128), BF16), jnp.zeros((128, 128), BF16)))
    return jnp.concatenate(left, axis=1), jnp.concatenate(right, axis=1)


def merges(keys, loads, tops):
    lane = lax.broadcasted_iota(I32, (8, 128), 1)
    sub = lax.broadcasted_iota(I32, (8, 128), 0)

    def bit(b):
        if b < 4 or b >= 14:
            return None
        where = sub >> (b - 4) if b < 7 else lane >> (b - 7)
        return (where & 1) == 1

    for top in tops:
        for b in range(top - 1, -1, -1):
            down = bit(top)
            new_k, new_w = list(keys), list(loads)
            if b < 4:
                for v in range(16):
                    if (v >> b) & 1:
                        continue
                    u = v | (1 << b)
                    if top < 4 and (v >> top) & 1:
                        swap = keys[v] < keys[u]
                    else:
                        swap = keys[v] > keys[u]
                    if down is not None:
                        swap = jnp.logical_xor(swap, down)
                    new_k[v] = jnp.where(swap, keys[u], keys[v])
                    new_k[u] = jnp.where(swap, keys[v], keys[u])
                    new_w[v] = jnp.where(swap, loads[u], loads[v])
                    new_w[u] = jnp.where(swap, loads[v], loads[u])
            else:
                keep_max = bit(b) if down is None else jnp.logical_xor(bit(b), down)
                if b < 7:
                    idx, axis = sub ^ (1 << (b - 4)), 0
                else:
                    idx, axis = lane ^ (1 << (b - 7)), 1
                for v in range(16):
                    k, w = keys[v], loads[v]
                    pk = jnp.take_along_axis(k, idx, axis=axis, mode="promise_in_bounds")
                    pw = jnp.take_along_axis(w, idx, axis=axis, mode="promise_in_bounds")
                    take = jnp.logical_or(
                        jnp.logical_and(keep_max, pk > k),
                        jnp.logical_and(jnp.logical_not(keep_max), pk < k),
                    )
                    new_k[v] = jnp.where(take, pk, k)
                    new_w[v] = jnp.where(take, pw, w)
            keys, loads = new_k, new_w
    return keys, loads


def whole_kernel(
    n_lat, n_lon,
    temp_hbm, salt_hbm, east_hbm, north_hbm, vdiff_hbm, kmt_hbm, owner_hbm, cell_hbm, weight_hbm,
    t_ref, s_ref, atmo_ref,
    tp, sp, vp, up, vd, inv, gain, back_ref, c_mid, c_east, c_west, c_north, c_south,
    row_up, row_down, col_out, row_up2, row_down2, col_out2,
    g_north, g_south, g_west, g_east, g_north2, g_south2, g_west2, g_east2,
    edge, kp, kmt_ref, owner_ref, cell_ref, weight_ref, key_ref, load_ref, surf_ref, send, recv,
    load_sem, send_sem, recv_sem, ready, all_send, all_recv,
):
    n = n_lat * n_lon
    lat, lon = lax.axis_index("lat"), lax.axis_index("lon")
    me = lat * n_lon + lon
    is_top = lat == n_lat - 1
    has_south = lat > 0
    north_id = (jnp.where(is_top, lat, lat + 1), jnp.where(is_top, n_lon - 1 - lon, lon))
    south_id = (jnp.maximum(lat - 1, 0), lon)
    east_id = (lat, lax.rem(lon + 1, n_lon))
    west_id = (lat, lax.rem(lon + n_lon - 1, n_lon))

    loads = [
        pltpu.make_async_copy(src, dst, load_sem.at[i])
        for i, (src, dst) in enumerate(
            (
                (kmt_hbm, kmt_ref),
                (temp_hbm, tp.at[:, 8:40, :]),
                (salt_hbm, sp.at[:, 8:40, :]),
                (east_hbm, up),
                (north_hbm, vp.at[:, 8:40, :]),
                (vdiff_hbm, vd),
                (owner_hbm, owner_ref),
                (cell_hbm, cell_ref),
                (weight_hbm, weight_ref),
            )
        )
    ]
    for load in loads:
        load.start()

    barrier = pltpu.get_barrier_semaphore()

    def greet_row(sem):
        def one(d, _):
            peer = (lat, lax.rem(lon + d, n_lon))
            pl.semaphore_signal(sem, inc=1, device_id=peer, device_id_type=MESH)
            return 0

        lax.fori_loop(1, n_lon, one, 0)

    def greet_column(d, _):
        peer = (lax.rem(lat + d, n_lat), lon)
        pl.semaphore_signal(barrier, inc=1, device_id=peer, device_id_type=MESH)
        return 0

    lax.fori_loop(1, n_lat, greet_column, 0)
    greet_row(barrier)

    @pl.when(jnp.logical_not(has_south))
    def _():
        g_south[...] = jnp.zeros_like(g_south)
        g_south2[...] = jnp.zeros_like(g_south2)

    lane = lax.broadcasted_iota(I32, (32, 128), 1)
    lane8 = lax.broadcasted_iota(I32, (8, 128), 1)
    sub8 = lax.broadcasted_iota(I32, (8, 128), 0)
    loads[0].wait()
    kmt = kmt_ref[...].astype(F32)
    kp[8:40, :] = kmt

    def take_rows(src, row, dst, base):
        for g in range(8):
            dst[base + 8 * g : base + 8 * g + 8, :] = src[8 * g : 8 * g + 8, row, :]

    def put_rows(value, dst, g, row):
        dst[8 * g : 8 * g + 8, row, :] = value

    for load in loads[1:5]:
        load.wait()
    for base, src in ((0, tp), (64, sp), (136, vp)):
        take_rows(src, 39, row_up, base)
    for base, src in ((0, tp), (64, sp)):
        take_rows(src, 8, row_down, base)
    row_up[128:136, :] = jnp.broadcast_to(kp[39:40, :], (8, 128))
    row_down[128:136, :] = jnp.broadcast_to(kp[8:9, :], (8, 128))

    def pack_level(k, packs):
        pair = (lane >> 1) == k
        fields = (tp[k, 8:40, :], sp[k, 8:40, :], up[k])
        return tuple(
            jnp.where(pair, at_lane(x, 2 * k + 1), p) for x, p in zip(fields, packs)
        )

    zero = jnp.zeros((32, 128), F32)
    packs = lax.fori_loop(0, 64, pack_level, (zero, zero, zero), unroll=16)
    col_out[0:32, :] = packs[0]
    col_out[32:64, :] = packs[1]
    col_out[64:96, :] = at_lane(kmt, 1)
    col_out[96:128, :] = packs[2]

    pl.semaphore_wait(barrier, n_lat + n_lon - 2)

    def exchange(base, up_rows, top_rows, down_rows, east_rows, west_rows, bufs, ghosts):
        row_n, row_s, col = bufs
        north, south, west, east = ghosts

        def copy(src, dst, which, slot, peer):
            return pltpu.make_async_remote_copy(
                src_ref=src, dst_ref=dst, send_sem=send_sem.at[base + which],
                recv_sem=recv_sem.at[base + slot], device_id=peer, device_id_type=MESH,
            )

        to_north = copy(row_n.at[0:up_rows], south.at[0:up_rows], 0, 1, north_id)
        over_fold = copy(row_n.at[0:top_rows], north.at[0:top_rows], 0, 0, north_id)
        to_south = copy(row_s.at[0:down_rows], north.at[0:down_rows], 1, 0, south_id)
        to_east = copy(col.at[0:east_rows], west.at[0:east_rows], 2, 2, east_id)
        to_west = copy(col.at[0:west_rows], east.at[0:west_rows], 3, 3, west_id)

        def start():
            @pl.when(is_top)
            def _():
                over_fold.start()

            @pl.when(jnp.logical_not(is_top))
            def _():
                to_north.start()

            @pl.when(has_south)
            def _():
                to_south.start()

            to_east.start()
            to_west.start()

        def finish():
            @pl.when(is_top)
            def _():
                over_fold.wait_send()

            @pl.when(jnp.logical_not(is_top))
            def _():
                to_north.wait_send()

            @pl.when(has_south)
            def _():
                to_south.wait_send()
                to_north.wait_recv()

            to_south.wait_recv()
            to_east.wait()
            to_west.wait()

        return start, finish

    start, finish = exchange(
        0, 200, 136, 136, 128, 96, (row_up, row_down, col_out), (g_north, g_south, g_west, g_east)
    )
    start()
    greet_row(ready)

    loads[5].wait()

    def factor(k, carry):
        above, back = carry
        below = jnp.where((k + 1).astype(F32) < kmt, vd[k], 0.0)
        whole = 1.0 / (1.0 + below + above - above * back)
        inv[k] = whole
        gain[k] = above * whole
        back = below * whole
        back_ref[k] = back
        return below, back

    lax.fori_loop(0, 64, factor, (zero, zero), unroll=4)

    for load in loads[6:]:
        load.wait()

    def hold(keys, loads):
        for v in range(16):
            key_ref[8 * v : 8 * v + 8, :] = keys[v]
            load_ref[8 * v : 8 * v + 8, :] = loads[v]

    def held(ref):
        return [ref[8 * v : 8 * v + 8, :] for v in range(16)]

    keys, shares = [], []
    for l in range(4):
        for j in range(4):
            rows = slice(8 * j, 8 * j + 8)
            place = (8 * j + sub8) * 128 + lane8
            keys.append((owner_ref[l, rows, :] << 23) | (cell_ref[l, rows, :] << 12) | place)
            shares.append(weight_ref[l, rows, :])
    hold(*merges(keys, shares, range(1, FIRST_MERGES + 1)))

    finish()

    mirror = jnp.where(is_top, 127 - lane8, lane8)

    def ghost_rows(north, south, fields):
        for base, dst in fields:
            for g in range(8):
                rows = slice(base + 8 * g, base + 8 * g + 8)
                put_rows(lanes_of(north[rows, :], mirror), dst, g, 40)
                put_rows(south[rows, :], dst, g, 7)

    def ghost_cols(west, east, count):
        for i in range(count):
            rows = slice(32 * i, 32 * i + 32)
            edge[rows, :] = jnp.where(
                (lane & 1) == 0, west[rows, :], at_lane(east[rows, :], 126)
            )

    ghost_rows(g_north, g_south, ((0, tp), (64, sp)))
    for g in range(8):
        put_rows(g_south[136 + 8 * g : 144 + 8 * g, :], vp, g, 7)
    kp[40:48, :] = lanes_of(g_north[128:136, :], mirror)
    kp[0:8, :] = g_south[128:136, :]
    ghost_cols(g_west, g_east, 3)
    edge[96:128, :] = g_west[96:128, :]

    first, last = lane == 0, lane == 127
    kmt_edge = edge[64:96, :]
    wet_east = jnp.minimum(kmt, jnp.where(last, kmt_edge, at_lane(kmt, 127)))
    wet_west = jnp.minimum(kmt, jnp.where(first, kmt_edge, at_lane(kmt, 1)))
    wet_north = jnp.minimum(kmt, kp[9:41, :])
    wet_south = jnp.minimum(kmt, kp[7:39, :])

    def stencil(src, row, k, turn, coefs):
        mid, east, west, north, south = coefs
        here = src[k, 8:40, :]
        ghost = at_lane(edge[row : row + 32, :], turn)
        on_east = jnp.where(last, ghost, at_lane(here, 127))
        on_west = jnp.where(first, ghost, at_lane(here, 1))
        return (
            mid * here + east * on_east + west * on_west
            + north * src[k, 9:41, :] + south * src[k, 7:39, :]
        )

    def advance(k, carry, turn, coefs):
        above = gain[k]
        ft = stencil(tp, 0, k, turn, coefs) + above * carry[0]
        fs = stencil(sp, 32, k, turn, coefs) + above * carry[1]
        t_ref[k] = ft
        s_ref[k] = fs
        return ft, fs

    def down_first(k, carry):
        turn = lax.rem(128 - 2 * k, 128)
        level = k.astype(F32)
        whole = inv[k]
        half_e = 0.5 * up[k]
        half_w = jnp.where(first, 0.5 * at_lane(edge[96:128, :], turn), at_lane(half_e, 1))
        half_n = 0.5 * vp[k, 8:40, :]
        half_s = 0.5 * vp[k, 7:39, :]
        on_e, on_w = level < wet_east, level < wet_west
        on_n, on_s = level < wet_north, level < wet_south
        east = jnp.where(on_e, mixing - half_e, 0.0)
        west = jnp.where(on_w, mixing + half_w, 0.0)
        north = jnp.where(on_n, mixing - half_n, 0.0)
        south = jnp.where(on_s, mixing + half_s, 0.0)
        faces = (
            jnp.where(on_e, 2 * mixing, 0.0) + jnp.where(on_w, 2 * mixing, 0.0)
        ) + (jnp.where(on_n, 2 * mixing, 0.0) + jnp.where(on_s, 2 * mixing, 0.0))
        mid = (1.0 + (((east + west) + (north + south)) - faces)) * whole
        east, west, north, south = east * whole, west * whole, north * whole, south * whole
        c_mid[k], c_east[k], c_west[k], c_north[k], c_south[k] = mid, east, west, north, south
        return advance(k, carry, turn, (mid, east, west, north, south))

    lax.fori_loop(0, 64, down_first, (zero, zero), unroll=16)

    def up_first(i, carry):
        xt, xs, pack_t, pack_s = carry
        k = 63 - i
        back = back_ref[k]
        xt = t_ref[k] + back * xt
        xs = s_ref[k] + back * xs
        tp[k, 8:40, :] = xt
        sp[k, 8:40, :] = xs
        pair = (lane >> 1) == k
        pack_t = jnp.where(pair, at_lane(xt, 2 * k + 1), pack_t)
        pack_s = jnp.where(pair, at_lane(xs, 2 * k + 1), pack_s)
        return xt, xs, pack_t, pack_s

    _, _, pack_t, pack_s = lax.fori_loop(0, 64, up_first, (zero, zero, zero, zero), unroll=16)
    col_out2[0:32, :] = pack_t
    col_out2[32:64, :] = pack_s
    for base, src in ((0, tp), (64, sp)):
        take_rows(src, 39, row_up2, base)
        take_rows(src, 8, row_down2, base)

    start, finish = exchange(
        4, 128, 128, 128, 64, 64,
        (row_up2, row_down2, col_out2), (g_north2, g_south2, g_west2, g_east2),
    )
    start()

    keys, shares = merges(held(key_ref), held(load_ref), range(FIRST_MERGES + 1, 15))
    hold(keys, shares)
    begin = owner_starts(keys)
    cells = owner_slots([((k >> 12) & 2047).astype(F32) for k in keys], begin)
    for c in range(4):
        send[:, 8 + c, :] = jnp.concatenate(cells[c], axis=0).T

    finish()
    ghost_rows(g_north2, g_south2, ((0, tp), (64, sp)))
    ghost_cols(g_west2, g_east2, 2)

    def down_second(k, carry):
        turn = lax.rem(128 - 2 * k, 128)
        return advance(k, carry, turn, (c_mid[k], c_east[k], c_west[k], c_north[k], c_south[k]))

    lax.fori_loop(0, 64, down_second, (zero, zero), unroll=16)

    def up_second(i, carry):
        k = 63 - i
        back = back_ref[k]
        xt = t_ref[k] + back * carry[0]
        xs = s_ref[k] + back * carry[1]
        t_ref[k] = xt
        s_ref[k] = xs
        return xt, xs

    xt, xs = lax.fori_loop(0, 64, up_second, (zero, zero), unroll=16)
    wet = jnp.where(kmt > 0.0, 1.0, 0.0)
    surf_ref[0] = xt * wet
    surf_ref[1] = xs * wet

    values = link_values(surf_ref, key_ref, load_ref)
    count = jnp.where(lane8 < 127, pltpu.roll(begin, 127, 1), 16384) - begin
    for f in range(2):
        slots = owner_slots(values[f], begin)
        for c in range(4):
            kept = [
                jnp.where(sub8 * 16 + (c * 128 + v) < count, slots[c][v], 0.0) for v in range(16)
            ]
            send[:, 4 * f + c, :] = jnp.concatenate(kept, axis=0).T

    pl.semaphore_wait(ready, n_lon - 1)

    def send_one(d, _):
        to = lax.rem(me + d, n)
        pltpu.make_async_remote_copy(
            src_ref=send.at[to], dst_ref=recv.at[d], send_sem=all_send,
            recv_sem=all_recv.at[d // GROUP],
            device_id=(to // n_lon, lax.rem(to, n_lon)), device_id_type=MESH,
        ).start()
        return 0

    lax.fori_loop(1, n, send_one, 0)
    recv[0] = send[me]

    def add_group(g, total):
        @pl.when(g == 0)
        def _():
            part = recv.at[1:GROUP]
            pltpu.make_async_copy(part, part, all_recv.at[0]).wait()

        @pl.when(g > 0)
        def _():
            part = recv.at[pl.ds(pl.multiple_of(g * GROUP, GROUP), GROUP)]
            pltpu.make_async_copy(part, part, all_recv.at[g]).wait()

        left, right = group_operands(recv, g * GROUP)
        return total + lax.dot_general(
            right, left, (((1,), (1,)), ((), ())), preferred_element_type=F32
        )

    total = lax.fori_loop(0, n // GROUP, add_group, jnp.zeros((128, 64), F32))
    write_sums(total.T, atmo_ref)
    sent = send.at[0 : n - 1]
    pltpu.make_async_copy(sent, sent, all_send).wait()


def whole_call(n_lat, n_lon, *arrays):
    vm = pl.BlockSpec(memory_space=pltpu.VMEM)
    hbm = pl.BlockSpec(memory_space=pltpu.HBM)
    field = jax.ShapeDtypeStruct((64, 32, 128), F32)
    block, wide = pltpu.VMEM((64, 32, 128), F32), pltpu.VMEM((64, 48, 128), F32)
    links = pltpu.VMEM((4, 32, 128), I32)
    dma = pltpu.SemaphoreType.DMA
    n = n_lat * n_lon

    def rows(count, dtype=F32):
        return pltpu.VMEM((count, 128), dtype)

    return pl.pallas_call(
        functools.partial(whole_kernel, n_lat, n_lon),
        out_shape=(field, field, jax.ShapeDtypeStruct((2, 2048), F32)),
        in_specs=[hbm] * 9,
        out_specs=(vm,) * 3,
        scratch_shapes=[wide] * 3
        + [block] * 10
        + [rows(r) for r in (200, 136, 128, 128, 128, 64)]
        + [rows(r) for r in (136, 200, 128, 96, 128, 128, 64, 64)]
        + [rows(128), rows(48), pltpu.VMEM((32, 128), I32), links, links, pltpu.VMEM((4, 32, 128), F32)]
        + [rows(128, I32), rows(128), pltpu.VMEM((2, 32, 128), F32)]
        + [pltpu.VMEM((128, 12, 128), F32)] * 2
        + [dma((9,)), dma((8,)), dma((8,)), pltpu.SemaphoreType.REGULAR, dma, dma((n // GROUP,))],
        compiler_params=pltpu.CompilerParams(
            collective_id=1, has_side_effects=True, vmem_limit_bytes=VMEM_MB << 20
        ),
    )(*(pltpu.with_memory_space_constraint(a, pltpu.HBM) for a in arrays))


def hand_kernel(t_in, s_in, atmo_in, t_out, s_out, atmo_out, sem):
    puts = [
        pltpu.make_async_copy(src, dst, sem.at[i])
        for i, (src, dst) in enumerate(((t_in, t_out), (s_in, s_out), (atmo_in, atmo_out)))
    ]
    for put in puts:
        put.start()
    for put in puts:
        put.wait()


def hand_call(temp, salt, atmo):
    hbm = pl.BlockSpec(memory_space=pl.ANY)
    shapes = [jax.ShapeDtypeStruct(a.shape, a.dtype) for a in (temp, salt, atmo)]
    return pl.pallas_call(
        hand_kernel,
        out_shape=tuple(shapes),
        in_specs=[pl.BlockSpec(memory_space=pltpu.VMEM)] * 3,
        out_specs=(hbm,) * 3,
        scratch_shapes=[pltpu.SemaphoreType.DMA((3,))],
        compiler_params=pltpu.CompilerParams(vmem_limit_bytes=HAND_MB << 20),
    )(temp, salt, atmo)


def solution(mesh):
    n_lat, n_lon = mesh.shape["lat"], mesh.shape["lon"]
    level, flat = P(None, "lat", "lon"), P("lat", "lon")
    return jax.shard_map(
        lambda *a: hand_call(*whole_call(n_lat, n_lon, *a)),
        mesh=mesh,
        in_specs=(level,) * 5 + (flat,) + (level,) * 3,
        out_specs=(level, level, P(None, ("lat", "lon"))),
        check_vma=False,
    )
```

```python
import functools

import jax
import jax.numpy as jnp
from jax import lax
from jax.experimental import pallas as pl
from jax.experimental.pallas import tpu as pltpu
from jax.sharding import PartitionSpec as P

I32 = jnp.int32
F32 = jnp.float32
BF16 = jnp.bfloat16
MESH = pl.DeviceIdType.MESH
mixing = 0.1
GROUP = 16
FIRST_MERGES = 12
VMEM_MB = 32
HAND_MB = 8


def lanes_of(x, idx):
    return jnp.take_along_axis(x, idx, axis=1, mode="promise_in_bounds")


def owner_starts(keys):
    lane = lax.broadcasted_iota(I32, (8, 128), 1)
    first = jnp.broadcast_to(keys[0][0:1, :], (8, 128))
    bound = lane << 23
    count = jnp.zeros((8, 128), I32)
    for step in (128, 64, 32, 16, 8, 4, 2, 1):
        trial = count + step
        value = lanes_of(first, jnp.minimum(trial - 1, 127))
        fits = jnp.logical_and(trial <= 128, value < bound)
        count = jnp.where(fits, trial, count)
    column = jnp.maximum(count - 1, 0)
    within = jnp.zeros((8, 128), I32)
    for v in range(16):
        within = within + jnp.where(lanes_of(keys[v], column) < bound, 1, 0)
    within = jnp.broadcast_to(jnp.sum(within, axis=0, keepdims=True), (8, 128))
    return jnp.where(count > 0, column * 128 + within, 0)


def owner_slots(tiles, start):
    sub = lax.broadcasted_iota(I32, (8, 128), 0)
    column = start >> 7
    turn = start & 127
    x = []
    for c in range(5):
        idx = jnp.minimum(column + c, 127)
        x.append([lanes_of(tiles[v], idx) for v in range(16)])
    for n in (64, 32, 16):
        on = (turn & n) != 0
        a = n // 16
        low = sub < 8 - a
        rolled = [[pltpu.roll(t, 8 - a, 0) for t in row] for row in x]
        x = [
            [
                jnp.where(on, jnp.where(low, rolled[c][v], rolled[min(c + 1, 4)][v]), x[c][v])
                for v in range(16)
            ]
            for c in range(5)
        ]
    low = sub < 7
    for n in (8, 4, 2, 1):
        on = (turn & n) != 0
        rolled = [[pltpu.roll(row[v], 7, 0) for v in range(n)] for row in x]
        out = []
        for c in range(5 if n > 1 else 4):
            row = []
            for v in range(16):
                if v + n < 16:
                    moved = x[c][v + n]
                else:
                    moved = jnp.where(low, rolled[c][v + n - 16], rolled[min(c + 1, 4)][v + n - 16])
                row.append(jnp.where(on, moved, x[c][v]))
            out.append(row)
        x = out
    return x


def link_values(surf_ref, key_ref, load_ref):
    keys = [key_ref[pl.ds(8 * v, 8), :] for v in range(16)]
    lanes = [k & 127 for k in keys]
    rows = [(k >> 7) & 31 for k in keys]
    found = [[jnp.zeros((8, 128), F32)] * 16 for _ in range(2)]
    for r in range(32):
        table = [jnp.broadcast_to(surf_ref[f, r : r + 1, :], (8, 128)) for f in range(2)]
        for v in range(16):
            here = rows[v] == r
            for f in range(2):
                found[f][v] = jnp.where(here, lanes_of(table[f], lanes[v]), found[f][v])
    loads = [load_ref[pl.ds(8 * v, 8), :] for v in range(16)]
    return [[loads[v] * found[f][v] for v in range(16)] for f in range(2)]


def write_sums(total, out_ref):
    for f in range(2):
        summed = total[32 * f : 32 * f + 16] + total[32 * f + 16 : 32 * f + 32]
        for h in range(16):
            out_ref[f : f + 1, 128 * h : 128 * h + 128] = summed[h : h + 1]


def at_lane(x, shift):
    return pltpu.roll(x, shift, 1)


def group_operands(recv_ref, cell_ref, first):
    high_id = lax.broadcasted_iota(I32, (16, 128), 0).astype(F32).astype(BF16)
    low_id = lax.broadcasted_iota(I32, (128, 128), 0).astype(F32).astype(BF16)
    left, right = [], []
    for q in range(GROUP):
        cell = cell_ref[first + q]
        high = jnp.floor(cell * (1.0 / 128.0))
        low = cell - 128.0 * high
        values = recv_ref[first + q]
        coarse = values.astype(BF16).astype(F32)
        fine = values - coarse
        for c in range(4):
            hits = jnp.broadcast_to(high[c : c + 1], (16, 128)).astype(BF16) == high_id
            part = []
            for f in range(2):
                for piece in (coarse, fine):
                    row = jnp.broadcast_to(piece[4 * f + c : 4 * f + c + 1], (16, 128)).astype(BF16)
                    part.append(jnp.where(hits, row, jnp.zeros_like(row)))
            left.append(jnp.concatenate(part, axis=0))
            match = jnp.broadcast_to(low[c : c + 1], (128, 128)).astype(BF16) == low_id
            right.append(jnp.where(match, jnp.ones((128, 128), BF16), jnp.zeros((128, 128), BF16)))
    return jnp.concatenate(left, axis=1), jnp.concatenate(right, axis=1)


def merges(keys, loads, tops):
    lane = lax.broadcasted_iota(I32, (8, 128), 1)
    sub = lax.broadcasted_iota(I32, (8, 128), 0)

    def bit(b):
        if b < 4 or b >= 14:
            return None
        where = sub >> (b - 4) if b < 7 else lane >> (b - 7)
        return (where & 1) == 1

    for top in tops:
        for b in range(top - 1, -1, -1):
            down = bit(top)
            new_k, new_w = list(keys), list(loads)
            if b < 4:
                for v in range(16):
                    if (v >> b) & 1:
                        continue
                    u = v | (1 << b)
                    if top < 4 and (v >> top) & 1:
                        swap = keys[v] < keys[u]
                    else:
                        swap = keys[v] > keys[u]
                    if down is not None:
                        swap = jnp.logical_xor(swap, down)
                    new_k[v] = jnp.where(swap, keys[u], keys[v])
                    new_k[u] = jnp.where(swap, keys[v], keys[u])
                    new_w[v] = jnp.where(swap, loads[u], loads[v])
                    new_w[u] = jnp.where(swap, loads[v], loads[u])
            else:
                keep_max = bit(b) if down is None else jnp.logical_xor(bit(b), down)
                if b < 7:
                    idx, axis = sub ^ (1 << (b - 4)), 0
                else:
                    idx, axis = lane ^ (1 << (b - 7)), 1
                for v in range(16):
                    k, w = keys[v], loads[v]
                    pk = jnp.take_along_axis(k, idx, axis=axis, mode="promise_in_bounds")
                    pw = jnp.take_along_axis(w, idx, axis=axis, mode="promise_in_bounds")
                    take = jnp.logical_or(
                        jnp.logical_and(keep_max, pk > k),
                        jnp.logical_and(jnp.logical_not(keep_max), pk < k),
                    )
                    new_k[v] = jnp.where(take, pk, k)
                    new_w[v] = jnp.where(take, pw, w)
            keys, loads = new_k, new_w
    return keys, loads


def whole_kernel(
    n_lat, n_lon,
    temp_hbm, salt_hbm, east_hbm, north_hbm, vdiff_hbm, kmt_hbm, owner_hbm, cell_hbm, weight_hbm,
    t_ref, s_ref, atmo_ref,
    tp, sp, vp, up, vd, inv, gain, back_ref, c_mid, c_east, c_west, c_north, c_south,
    row_up, row_down, col_out, row_up2, row_down2, col_out2,
    g_north, g_south, g_west, g_east, g_north2, g_south2, g_west2, g_east2,
    edge, kp, kmt_ref, owner_ref, cell_ref, weight_ref, key_ref, load_ref, surf_ref, send, recv, send_cells, recv_cells,
    load_sem, send_sem, recv_sem, ready, all_send, all_recv, cells_send, cells_recv,
):
    n = n_lat * n_lon
    lat, lon = lax.axis_index("lat"), lax.axis_index("lon")
    me = lat * n_lon + lon
    is_top = lat == n_lat - 1
    has_south = lat > 0
    north_id = (jnp.where(is_top, lat, lat + 1), jnp.where(is_top, n_lon - 1 - lon, lon))
    south_id = (jnp.maximum(lat - 1, 0), lon)
    east_id = (lat, lax.rem(lon + 1, n_lon))
    west_id = (lat, lax.rem(lon + n_lon - 1, n_lon))

    loads = [
        pltpu.make_async_copy(src, dst, load_sem.at[i])
        for i, (src, dst) in enumerate(
            (
                (kmt_hbm, kmt_ref),
                (temp_hbm, tp.at[:, 8:40, :]),
                (salt_hbm, sp.at[:, 8:40, :]),
                (east_hbm, up),
                (north_hbm, vp.at[:, 8:40, :]),
                (vdiff_hbm, vd),
                (owner_hbm, owner_ref),
                (cell_hbm, cell_ref),
                (weight_hbm, weight_ref),
            )
        )
    ]
    for load in loads:
        load.start()

    barrier = pltpu.get_barrier_semaphore()

    def greet_row(sem):
        def one(d, _):
            peer = (lat, lax.rem(lon + d, n_lon))
            pl.semaphore_signal(sem, inc=1, device_id=peer, device_id_type=MESH)
            return 0

        lax.fori_loop(1, n_lon, one, 0)

    def greet_column(d, _):
        peer = (lax.rem(lat + d, n_lat), lon)
        pl.semaphore_signal(barrier, inc=1, device_id=peer, device_id_type=MESH)
        return 0

    lax.fori_loop(1, n_lat, greet_column, 0)
    greet_row(barrier)

    @pl.when(jnp.logical_not(has_south))
    def _():
        g_south[...] = jnp.zeros_like(g_south)
        g_south2[...] = jnp.zeros_like(g_south2)

    lane = lax.broadcasted_iota(I32, (32, 128), 1)
    lane8 = lax.broadcasted_iota(I32, (8, 128), 1)
    sub8 = lax.broadcasted_iota(I32, (8, 128), 0)
    loads[0].wait()
    kmt = kmt_ref[...].astype(F32)
    kp[8:40, :] = kmt

    def take_rows(src, row, dst, base):
        for g in range(8):
            dst[base + 8 * g : base + 8 * g + 8, :] = src[8 * g : 8 * g + 8, row, :]

    def put_rows(value, dst, g, row):
        dst[8 * g : 8 * g + 8, row, :] = value

    for load in loads[1:5]:
        load.wait()
    for base, src in ((0, tp), (64, sp), (136, vp)):
        take_rows(src, 39, row_up, base)
    for base, src in ((0, tp), (64, sp)):
        take_rows(src, 8, row_down, base)
    row_up[128:136, :] = jnp.broadcast_to(kp[39:40, :], (8, 128))
    row_down[128:136, :] = jnp.broadcast_to(kp[8:9, :], (8, 128))

    def pack_level(k, packs):
        pair = (lane >> 1) == k
        fields = (tp[k, 8:40, :], sp[k, 8:40, :], up[k])
        return tuple(
            jnp.where(pair, at_lane(x, 2 * k + 1), p) for x, p in zip(fields, packs)
        )

    zero = jnp.zeros((32, 128), F32)
    packs = lax.fori_loop(0, 64, pack_level, (zero, zero, zero), unroll=32)
    col_out[0:32, :] = packs[0]
    col_out[32:64, :] = packs[1]
    col_out[64:96, :] = at_lane(kmt, 1)
    col_out[96:128, :] = packs[2]

    pl.semaphore_wait(barrier, n_lat + n_lon - 2)

    def exchange(base, up_rows, top_rows, down_rows, east_rows, west_rows, bufs, ghosts):
        row_n, row_s, col = bufs
        north, south, west, east = ghosts

        def copy(src, dst, which, slot, peer):
            return pltpu.make_async_remote_copy(
                src_ref=src, dst_ref=dst, send_sem=send_sem.at[base + which],
                recv_sem=recv_sem.at[base + slot], device_id=peer, device_id_type=MESH,
            )

        to_north = copy(row_n.at[0:up_rows], south.at[0:up_rows], 0, 1, north_id)
        over_fold = copy(row_n.at[0:top_rows], north.at[0:top_rows], 0, 0, north_id)
        to_south = copy(row_s.at[0:down_rows], north.at[0:down_rows], 1, 0, south_id)
        to_east = copy(col.at[0:east_rows], west.at[0:east_rows], 2, 2, east_id)
        to_west = copy(col.at[0:west_rows], east.at[0:west_rows], 3, 3, west_id)

        def start():
            @pl.when(is_top)
            def _():
                over_fold.start()

            @pl.when(jnp.logical_not(is_top))
            def _():
                to_north.start()

            @pl.when(has_south)
            def _():
                to_south.start()

            to_east.start()
            to_west.start()

        def finish():
            @pl.when(is_top)
            def _():
                over_fold.wait_send()

            @pl.when(jnp.logical_not(is_top))
            def _():
                to_north.wait_send()

            @pl.when(has_south)
            def _():
                to_south.wait_send()
                to_north.wait_recv()

            to_south.wait_recv()
            to_east.wait()
            to_west.wait()

        return start, finish

    start, finish = exchange(
        0, 200, 136, 136, 128, 96, (row_up, row_down, col_out), (g_north, g_south, g_west, g_east)
    )
    start()
    greet_row(ready)

    loads[5].wait()

    def factor(k, carry):
        above, back = carry
        below = jnp.where((k + 1).astype(F32) < kmt, vd[k], 0.0)
        whole = 1.0 / (1.0 + below + above - above * back)
        inv[k] = whole
        gain[k] = above * whole
        back = below * whole
        back_ref[k] = back
        return below, back

    lax.fori_loop(0, 64, factor, (zero, zero), unroll=4)

    for load in loads[6:]:
        load.wait()

    def hold(keys, loads):
        for v in range(16):
            key_ref[8 * v : 8 * v + 8, :] = keys[v]
            load_ref[8 * v : 8 * v + 8, :] = loads[v]

    def held(ref):
        return [ref[8 * v : 8 * v + 8, :] for v in range(16)]

    keys, shares = [], []
    for l in range(4):
        for j in range(4):
            rows = slice(8 * j, 8 * j + 8)
            place = (8 * j + sub8) * 128 + lane8
            keys.append((owner_ref[l, rows, :] << 23) | (cell_ref[l, rows, :] << 12) | place)
            shares.append(weight_ref[l, rows, :])
    hold(*merges(keys, shares, range(1, FIRST_MERGES + 1)))

    finish()

    mirror = jnp.where(is_top, 127 - lane8, lane8)

    def ghost_rows(north, south, fields):
        for base, dst in fields:
            for g in range(8):
                rows = slice(base + 8 * g, base + 8 * g + 8)
                put_rows(lanes_of(north[rows, :], mirror), dst, g, 40)
                put_rows(south[rows, :], dst, g, 7)

    def ghost_cols(west, east, count):
        for i in range(count):
            rows = slice(32 * i, 32 * i + 32)
            edge[rows, :] = jnp.where(
                (lane & 1) == 0, west[rows, :], at_lane(east[rows, :], 126)
            )

    ghost_rows(g_north, g_south, ((0, tp), (64, sp)))
    for g in range(8):
        put_rows(g_south[136 + 8 * g : 144 + 8 * g, :], vp, g, 7)
    kp[40:48, :] = lanes_of(g_north[128:136, :], mirror)
    kp[0:8, :] = g_south[128:136, :]
    ghost_cols(g_west, g_east, 3)
    edge[96:128, :] = g_west[96:128, :]

    first, last = lane == 0, lane == 127
    kmt_edge = edge[64:96, :]
    wet_east = jnp.minimum(kmt, jnp.where(last, kmt_edge, at_lane(kmt, 127)))
    wet_west = jnp.minimum(kmt, jnp.where(first, kmt_edge, at_lane(kmt, 1)))
    wet_north = jnp.minimum(kmt, kp[9:41, :])
    wet_south = jnp.minimum(kmt, kp[7:39, :])

    def stencil(src, row, k, turn, coefs):
        mid, east, west, north, south = coefs
        here = src[k, 8:40, :]
        ghost = at_lane(edge[row : row + 32, :], turn)
        on_east = jnp.where(last, ghost, at_lane(here, 127))
        on_west = jnp.where(first, ghost, at_lane(here, 1))
        return (
            mid * here + east * on_east + west * on_west
            + north * src[k, 9:41, :] + south * src[k, 7:39, :]
        )

    def advance(k, carry, turn, coefs):
        above = gain[k]
        ft = stencil(tp, 0, k, turn, coefs) + above * carry[0]
        fs = stencil(sp, 32, k, turn, coefs) + above * carry[1]
        t_ref[k] = ft
        s_ref[k] = fs
        return ft, fs

    def down_first(k, carry):
        turn = lax.rem(128 - 2 * k, 128)
        level = k.astype(F32)
        whole = inv[k]
        half_e = 0.5 * up[k]
        half_w = jnp.where(first, 0.5 * at_lane(edge[96:128, :], turn), at_lane(half_e, 1))
        half_n = 0.5 * vp[k, 8:40, :]
        half_s = 0.5 * vp[k, 7:39, :]
        on_e, on_w = level < wet_east, level < wet_west
        on_n, on_s = level < wet_north, level < wet_south
        east = jnp.where(on_e, mixing - half_e, 0.0)
        west = jnp.where(on_w, mixing + half_w, 0.0)
        north = jnp.where(on_n, mixing - half_n, 0.0)
        south = jnp.where(on_s, mixing + half_s, 0.0)
        faces = (
            jnp.where(on_e, 2 * mixing, 0.0) + jnp.where(on_w, 2 * mixing, 0.0)
        ) + (jnp.where(on_n, 2 * mixing, 0.0) + jnp.where(on_s, 2 * mixing, 0.0))
        mid = (1.0 + (((east + west) + (north + south)) - faces)) * whole
        east, west, north, south = east * whole, west * whole, north * whole, south * whole
        c_mid[k], c_east[k], c_west[k], c_north[k], c_south[k] = mid, east, west, north, south
        return advance(k, carry, turn, (mid, east, west, north, south))

    lax.fori_loop(0, 64, down_first, (zero, zero), unroll=32)

    def up_first(i, carry):
        xt, xs, pack_t, pack_s = carry
        k = 63 - i
        back = back_ref[k]
        xt = t_ref[k] + back * xt
        xs = s_ref[k] + back * xs
        tp[k, 8:40, :] = xt
        sp[k, 8:40, :] = xs
        pair = (lane >> 1) == k
        pack_t = jnp.where(pair, at_lane(xt, 2 * k + 1), pack_t)
        pack_s = jnp.where(pair, at_lane(xs, 2 * k + 1), pack_s)
        return xt, xs, pack_t, pack_s

    _, _, pack_t, pack_s = lax.fori_loop(0, 64, up_first, (zero, zero, zero, zero), unroll=32)
    col_out2[0:32, :] = pack_t
    col_out2[32:64, :] = pack_s
    for base, src in ((0, tp), (64, sp)):
        take_rows(src, 39, row_up2, base)
        take_rows(src, 8, row_down2, base)

    start, finish = exchange(
        4, 128, 128, 128, 64, 64,
        (row_up2, row_down2, col_out2), (g_north2, g_south2, g_west2, g_east2),
    )
    start()

    keys, shares = merges(held(key_ref), held(load_ref), range(FIRST_MERGES + 1, 15))
    hold(keys, shares)
    begin = owner_starts(keys)
    cells = owner_slots([((k >> 12) & 2047).astype(F32) for k in keys], begin)
    for c in range(4):
        send_cells[:, c, :] = jnp.concatenate(cells[c], axis=0).T

    pl.semaphore_wait(ready, n_lon - 1)

    def send_cell(d):
        to = lax.rem(me + d, n)
        pltpu.make_async_remote_copy(
            src_ref=send_cells.at[to], dst_ref=recv_cells.at[d], send_sem=cells_send,
            recv_sem=cells_recv,
            device_id=(to // n_lon, lax.rem(to, n_lon)), device_id_type=MESH,
        ).start()

    lax.fori_loop(1, n, lambda d, _: (send_cell(d), 0)[1], 0)

    finish()
    ghost_rows(g_north2, g_south2, ((0, tp), (64, sp)))
    ghost_cols(g_west2, g_east2, 2)

    def down_second(k, carry):
        turn = lax.rem(128 - 2 * k, 128)
        return advance(k, carry, turn, (c_mid[k], c_east[k], c_west[k], c_north[k], c_south[k]))

    lax.fori_loop(0, 64, down_second, (zero, zero), unroll=32)

    def up_second(i, carry):
        k = 63 - i
        back = back_ref[k]
        xt = t_ref[k] + back * carry[0]
        xs = s_ref[k] + back * carry[1]
        t_ref[k] = xt
        s_ref[k] = xs
        return xt, xs

    xt, xs = lax.fori_loop(0, 64, up_second, (zero, zero), unroll=32)
    wet = jnp.where(kmt > 0.0, 1.0, 0.0)
    surf_ref[0] = xt * wet
    surf_ref[1] = xs * wet

    values = link_values(surf_ref, key_ref, load_ref)
    count = jnp.where(lane8 < 127, pltpu.roll(begin, 127, 1), 16384) - begin
    for f in range(2):
        slots = owner_slots(values[f], begin)
        for c in range(4):
            kept = [
                jnp.where(sub8 * 16 + (c * 128 + v) < count, slots[c][v], 0.0) for v in range(16)
            ]
            send[:, 4 * f + c, :] = jnp.concatenate(kept, axis=0).T

    def send_one(d, _):
        to = lax.rem(me + d, n)
        pltpu.make_async_remote_copy(
            src_ref=send.at[to], dst_ref=recv.at[d], send_sem=all_send,
            recv_sem=all_recv.at[d // GROUP],
            device_id=(to // n_lon, lax.rem(to, n_lon)), device_id_type=MESH,
        ).start()
        return 0

    lax.fori_loop(1, n, send_one, 0)
    recv[0] = send[me]
    recv_cells[0] = send_cells[me]
    got = recv_cells.at[1:n]
    pltpu.make_async_copy(got, got, cells_recv).wait()

    def add_group(g, total):
        @pl.when(g == 0)
        def _():
            part = recv.at[1:GROUP]
            pltpu.make_async_copy(part, part, all_recv.at[0]).wait()

        @pl.when(g > 0)
        def _():
            part = recv.at[pl.ds(pl.multiple_of(g * GROUP, GROUP), GROUP)]
            pltpu.make_async_copy(part, part, all_recv.at[g]).wait()

        left, right = group_operands(recv, recv_cells, g * GROUP)
        return total + lax.dot_general(
            right, left, (((1,), (1,)), ((), ())), preferred_element_type=F32
        )

    total = lax.fori_loop(0, n // GROUP, add_group, jnp.zeros((128, 64), F32))
    write_sums(total.T, atmo_ref)
    sent = send.at[0 : n - 1]
    pltpu.make_async_copy(sent, sent, all_send).wait()
    sent = send_cells.at[0 : n - 1]
    pltpu.make_async_copy(sent, sent, cells_send).wait()


def whole_call(n_lat, n_lon, *arrays):
    vm = pl.BlockSpec(memory_space=pltpu.VMEM)
    hbm = pl.BlockSpec(memory_space=pltpu.HBM)
    field = jax.ShapeDtypeStruct((64, 32, 128), F32)
    block, wide = pltpu.VMEM((64, 32, 128), F32), pltpu.VMEM((64, 48, 128), F32)
    links = pltpu.VMEM((4, 32, 128), I32)
    dma = pltpu.SemaphoreType.DMA
    n = n_lat * n_lon

    def rows(count, dtype=F32):
        return pltpu.VMEM((count, 128), dtype)

    return pl.pallas_call(
        functools.partial(whole_kernel, n_lat, n_lon),
        out_shape=(field, field, jax.ShapeDtypeStruct((2, 2048), F32)),
        in_specs=[hbm] * 9,
        out_specs=(vm,) * 3,
        scratch_shapes=[wide] * 3
        + [block] * 10
        + [rows(r) for r in (200, 136, 128, 128, 128, 64)]
        + [rows(r) for r in (136, 200, 128, 96, 128, 128, 64, 64)]
        + [rows(128), rows(48), pltpu.VMEM((32, 128), I32), links, links, pltpu.VMEM((4, 32, 128), F32)]
        + [rows(128, I32), rows(128), pltpu.VMEM((2, 32, 128), F32)]
        + [pltpu.VMEM((128, 8, 128), F32)] * 2
        + [pltpu.VMEM((128, 4, 128), F32)] * 2
        + [dma((9,)), dma((8,)), dma((8,)), pltpu.SemaphoreType.REGULAR, dma, dma((n // GROUP,)), dma, dma],
        compiler_params=pltpu.CompilerParams(
            collective_id=1, has_side_effects=True, vmem_limit_bytes=VMEM_MB << 20
        ),
    )(*(pltpu.with_memory_space_constraint(a, pltpu.HBM) for a in arrays))


def hand_kernel(t_in, s_in, atmo_in, t_out, s_out, atmo_out, sem):
    puts = [
        pltpu.make_async_copy(src, dst, sem.at[i])
        for i, (src, dst) in enumerate(((t_in, t_out), (s_in, s_out), (atmo_in, atmo_out)))
    ]
    for put in puts:
        put.start()
    for put in puts:
        put.wait()


def hand_call(temp, salt, atmo):
    hbm = pl.BlockSpec(memory_space=pl.ANY)
    shapes = [jax.ShapeDtypeStruct(a.shape, a.dtype) for a in (temp, salt, atmo)]
    return pl.pallas_call(
        hand_kernel,
        out_shape=tuple(shapes),
        in_specs=[pl.BlockSpec(memory_space=pltpu.VMEM)] * 3,
        out_specs=(hbm,) * 3,
        scratch_shapes=[pltpu.SemaphoreType.DMA((3,))],
        compiler_params=pltpu.CompilerParams(vmem_limit_bytes=HAND_MB << 20),
    )(temp, salt, atmo)


def solution(mesh):
    n_lat, n_lon = mesh.shape["lat"], mesh.shape["lon"]
    level, flat = P(None, "lat", "lon"), P("lat", "lon")
    return jax.shard_map(
        lambda *a: hand_call(*whole_call(n_lat, n_lon, *a)),
        mesh=mesh,
        in_specs=(level,) * 5 + (flat,) + (level,) * 3,
        out_specs=(level, level, P(None, ("lat", "lon"))),
        check_vma=False,
    )
```

```python
import functools

import jax
import jax.numpy as jnp
from jax import lax
from jax.experimental import pallas as pl
from jax.experimental.pallas import tpu as pltpu
from jax.sharding import PartitionSpec as P

I32 = jnp.int32
F32 = jnp.float32
BF16 = jnp.bfloat16
MESH = pl.DeviceIdType.MESH
mixing = 0.1
GROUP = 16
FIRST_MERGES = 12
VMEM_MB = 32
HAND_MB = 8


def lanes_of(x, idx):
    return jnp.take_along_axis(x, idx, axis=1, mode="promise_in_bounds")


def owner_starts(keys):
    lane = lax.broadcasted_iota(I32, (8, 128), 1)
    first = jnp.broadcast_to(keys[0][0:1, :], (8, 128))
    bound = lane << 23
    count = jnp.zeros((8, 128), I32)
    for step in (128, 64, 32, 16, 8, 4, 2, 1):
        trial = count + step
        value = lanes_of(first, jnp.minimum(trial - 1, 127))
        fits = jnp.logical_and(trial <= 128, value < bound)
        count = jnp.where(fits, trial, count)
    column = jnp.maximum(count - 1, 0)
    within = jnp.zeros((8, 128), I32)
    for v in range(16):
        within = within + jnp.where(lanes_of(keys[v], column) < bound, 1, 0)
    within = jnp.broadcast_to(jnp.sum(within, axis=0, keepdims=True), (8, 128))
    return jnp.where(count > 0, column * 128 + within, 0)


def owner_slots(tiles, start):
    sub = lax.broadcasted_iota(I32, (8, 128), 0)
    column = start >> 7
    turn = start & 127
    x = []
    for c in range(5):
        idx = jnp.minimum(column + c, 127)
        x.append([lanes_of(tiles[v], idx) for v in range(16)])
    for n in (64, 32, 16):
        on = (turn & n) != 0
        a = n // 16
        low = sub < 8 - a
        rolled = [[pltpu.roll(t, 8 - a, 0) for t in row] for row in x]
        x = [
            [
                jnp.where(on, jnp.where(low, rolled[c][v], rolled[min(c + 1, 4)][v]), x[c][v])
                for v in range(16)
            ]
            for c in range(5)
        ]
    low = sub < 7
    for n in (8, 4, 2, 1):
        on = (turn & n) != 0
        rolled = [[pltpu.roll(row[v], 7, 0) for v in range(n)] for row in x]
        out = []
        for c in range(5 if n > 1 else 4):
            row = []
            for v in range(16):
                if v + n < 16:
                    moved = x[c][v + n]
                else:
                    moved = jnp.where(low, rolled[c][v + n - 16], rolled[min(c + 1, 4)][v + n - 16])
                row.append(jnp.where(on, moved, x[c][v]))
            out.append(row)
        x = out
    return x


def link_values(surf_ref, key_ref, load_ref):
    keys = [key_ref[pl.ds(8 * v, 8), :] for v in range(16)]
    lanes = [k & 127 for k in keys]
    rows = [(k >> 7) & 31 for k in keys]
    found = [[jnp.zeros((8, 128), F32)] * 16 for _ in range(2)]
    for r in range(32):
        table = [jnp.broadcast_to(surf_ref[f, r : r + 1, :], (8, 128)) for f in range(2)]
        for v in range(16):
            here = rows[v] == r
            for f in range(2):
                found[f][v] = jnp.where(here, lanes_of(table[f], lanes[v]), found[f][v])
    loads = [load_ref[pl.ds(8 * v, 8), :] for v in range(16)]
    return [[loads[v] * found[f][v] for v in range(16)] for f in range(2)]


def write_sums(total, out_ref):
    for f in range(2):
        summed = total[32 * f : 32 * f + 16] + total[32 * f + 16 : 32 * f + 32]
        for h in range(16):
            out_ref[f : f + 1, 128 * h : 128 * h + 128] = summed[h : h + 1]


def at_lane(x, shift):
    return pltpu.roll(x, shift, 1)


def group_operands(recv_ref, cell_ref, first):
    high_id = lax.broadcasted_iota(I32, (16, 128), 0).astype(F32).astype(BF16)
    low_id = lax.broadcasted_iota(I32, (128, 128), 0).astype(F32).astype(BF16)
    left, right = [], []
    for q in range(GROUP):
        cell = cell_ref[first + q]
        high = jnp.floor(cell * (1.0 / 128.0))
        low = cell - 128.0 * high
        values = recv_ref[first + q]
        coarse = values.astype(BF16).astype(F32)
        fine = values - coarse
        for c in range(4):
            hits = jnp.broadcast_to(high[c : c + 1], (16, 128)).astype(BF16) == high_id
            part = []
            for f in range(2):
                for piece in (coarse, fine):
                    row = jnp.broadcast_to(piece[4 * f + c : 4 * f + c + 1], (16, 128)).astype(BF16)
                    part.append(jnp.where(hits, row, jnp.zeros_like(row)))
            left.append(jnp.concatenate(part, axis=0))
            match = jnp.broadcast_to(low[c : c + 1], (128, 128)).astype(BF16) == low_id
            right.append(jnp.where(match, jnp.ones((128, 128), BF16), jnp.zeros((128, 128), BF16)))
    return jnp.concatenate(left, axis=1), jnp.concatenate(right, axis=1)


def merges(keys, loads, tops):
    lane = lax.broadcasted_iota(I32, (8, 128), 1)
    sub = lax.broadcasted_iota(I32, (8, 128), 0)

    def bit(b):
        if b < 4 or b >= 14:
            return None
        where = sub >> (b - 4) if b < 7 else lane >> (b - 7)
        return (where & 1) == 1

    for top in tops:
        for b in range(top - 1, -1, -1):
            down = bit(top)
            new_k, new_w = list(keys), list(loads)
            if b < 4:
                for v in range(16):
                    if (v >> b) & 1:
                        continue
                    u = v | (1 << b)
                    if top < 4 and (v >> top) & 1:
                        swap = keys[v] < keys[u]
                    else:
                        swap = keys[v] > keys[u]
                    if down is not None:
                        swap = jnp.logical_xor(swap, down)
                    new_k[v] = jnp.where(swap, keys[u], keys[v])
                    new_k[u] = jnp.where(swap, keys[v], keys[u])
                    new_w[v] = jnp.where(swap, loads[u], loads[v])
                    new_w[u] = jnp.where(swap, loads[v], loads[u])
            else:
                keep_max = bit(b) if down is None else jnp.logical_xor(bit(b), down)
                if b < 7:
                    idx, axis = sub ^ (1 << (b - 4)), 0
                else:
                    idx, axis = lane ^ (1 << (b - 7)), 1
                for v in range(16):
                    k, w = keys[v], loads[v]
                    pk = jnp.take_along_axis(k, idx, axis=axis, mode="promise_in_bounds")
                    pw = jnp.take_along_axis(w, idx, axis=axis, mode="promise_in_bounds")
                    take = jnp.logical_or(
                        jnp.logical_and(keep_max, pk > k),
                        jnp.logical_and(jnp.logical_not(keep_max), pk < k),
                    )
                    new_k[v] = jnp.where(take, pk, k)
                    new_w[v] = jnp.where(take, pw, w)
            keys, loads = new_k, new_w
    return keys, loads


def whole_kernel(
    n_lat, n_lon,
    temp_hbm, salt_hbm, east_hbm, north_hbm, vdiff_hbm, kmt_hbm, owner_hbm, cell_hbm, weight_hbm,
    t_ref, s_ref, atmo_ref,
    tp, sp, vp, up, vd, inv, gain, back_ref, c_mid, c_east, c_west, c_north, c_south,
    row_up, row_down, col_out, row_up2, row_down2, col_out2,
    g_north, g_south, g_west, g_east, g_north2, g_south2, g_west2, g_east2,
    edge, kp, kmt_ref, owner_ref, cell_ref, weight_ref, key_ref, load_ref, surf_ref, send, recv, send_cells, recv_cells,
    load_sem, send_sem, recv_sem, ready, all_send, all_recv, cells_send, cells_recv,
):
    n = n_lat * n_lon
    lat, lon = lax.axis_index("lat"), lax.axis_index("lon")
    me = lat * n_lon + lon
    is_top = lat == n_lat - 1
    has_south = lat > 0
    north_id = (jnp.where(is_top, lat, lat + 1), jnp.where(is_top, n_lon - 1 - lon, lon))
    south_id = (jnp.maximum(lat - 1, 0), lon)
    east_id = (lat, lax.rem(lon + 1, n_lon))
    west_id = (lat, lax.rem(lon + n_lon - 1, n_lon))

    loads = [
        pltpu.make_async_copy(src, dst, load_sem.at[i])
        for i, (src, dst) in enumerate(
            (
                (kmt_hbm, kmt_ref),
                (temp_hbm, tp.at[:, 8:40, :]),
                (salt_hbm, sp.at[:, 8:40, :]),
                (east_hbm, up),
                (north_hbm, vp.at[:, 8:40, :]),
                (vdiff_hbm, vd),
                (owner_hbm, owner_ref),
                (cell_hbm, cell_ref),
                (weight_hbm, weight_ref),
            )
        )
    ]
    for load in loads:
        load.start()

    barrier = pltpu.get_barrier_semaphore()

    def greet_row(sem):
        def one(d, _):
            peer = (lat, lax.rem(lon + d, n_lon))
            pl.semaphore_signal(sem, inc=1, device_id=peer, device_id_type=MESH)
            return 0

        lax.fori_loop(1, n_lon, one, 0)

    def greet_column(d, _):
        peer = (lax.rem(lat + d, n_lat), lon)
        pl.semaphore_signal(barrier, inc=1, device_id=peer, device_id_type=MESH)
        return 0

    lax.fori_loop(1, n_lat, greet_column, 0)
    greet_row(barrier)

    @pl.when(jnp.logical_not(has_south))
    def _():
        g_south[...] = jnp.zeros_like(g_south)
        g_south2[...] = jnp.zeros_like(g_south2)

    lane = lax.broadcasted_iota(I32, (32, 128), 1)
    lane8 = lax.broadcasted_iota(I32, (8, 128), 1)
    sub8 = lax.broadcasted_iota(I32, (8, 128), 0)
    loads[0].wait()
    kmt = kmt_ref[...].astype(F32)
    kp[8:40, :] = kmt

    def take_rows(src, row, dst, base):
        for g in range(8):
            dst[base + 8 * g : base + 8 * g + 8, :] = src[8 * g : 8 * g + 8, row, :]

    def put_rows(value, dst, g, row):
        dst[8 * g : 8 * g + 8, row, :] = value

    for load in loads[1:5]:
        load.wait()
    for base, src in ((0, tp), (64, sp), (136, vp)):
        take_rows(src, 39, row_up, base)
    for base, src in ((0, tp), (64, sp)):
        take_rows(src, 8, row_down, base)
    row_up[128:136, :] = jnp.broadcast_to(kp[39:40, :], (8, 128))
    row_down[128:136, :] = jnp.broadcast_to(kp[8:9, :], (8, 128))

    def pack_level(k, packs):
        pair = (lane >> 1) == k
        fields = (tp[k, 8:40, :], sp[k, 8:40, :], up[k])
        return tuple(
            jnp.where(pair, at_lane(x, 2 * k + 1), p) for x, p in zip(fields, packs)
        )

    zero = jnp.zeros((32, 128), F32)
    packs = lax.fori_loop(0, 64, pack_level, (zero, zero, zero), unroll=32)
    odd = (lane & 1) == 1

    def to_west_cols(pack_t, pack_s):
        return jnp.where(odd, pack_t, at_lane(pack_s, 127))

    def to_east_cols(pack_t, pack_s):
        return jnp.where(odd, at_lane(pack_s, 1), pack_t)

    col_out[0:32, :] = to_west_cols(packs[0], packs[1])
    col_out[32:64, :] = at_lane(kmt, 1)
    col_out[64:96, :] = to_east_cols(packs[0], packs[1])
    col_out[96:128, :] = packs[2]

    pl.semaphore_wait(barrier, n_lat + n_lon - 2)

    def exchange(base, up_rows, top_rows, down_rows, east_rows, west_rows, bufs, ghosts):
        row_n, row_s, col = bufs
        north, south, west, east = ghosts

        def copy(src, dst, which, slot, peer):
            return pltpu.make_async_remote_copy(
                src_ref=src, dst_ref=dst, send_sem=send_sem.at[base + which],
                recv_sem=recv_sem.at[base + slot], device_id=peer, device_id_type=MESH,
            )

        to_north = copy(row_n.at[0:up_rows], south.at[0:up_rows], 0, 1, north_id)
        over_fold = copy(row_n.at[0:top_rows], north.at[0:top_rows], 0, 0, north_id)
        to_south = copy(row_s.at[0:down_rows], north.at[0:down_rows], 1, 0, south_id)
        to_east = copy(col.at[32:east_rows], west.at[32:east_rows], 2, 2, east_id)
        to_west = copy(col.at[0:west_rows], east.at[0:west_rows], 3, 3, west_id)

        def start():
            @pl.when(is_top)
            def _():
                over_fold.start()

            @pl.when(jnp.logical_not(is_top))
            def _():
                to_north.start()

            @pl.when(has_south)
            def _():
                to_south.start()

            to_east.start()
            to_west.start()

        def finish():
            @pl.when(is_top)
            def _():
                over_fold.wait_send()

            @pl.when(jnp.logical_not(is_top))
            def _():
                to_north.wait_send()

            @pl.when(has_south)
            def _():
                to_south.wait_send()
                to_north.wait_recv()

            to_south.wait_recv()
            to_east.wait()
            to_west.wait()

        return start, finish

    start, finish = exchange(
        0, 200, 136, 136, 128, 64, (row_up, row_down, col_out), (g_north, g_south, g_west, g_east)
    )
    start()
    greet_row(ready)

    loads[5].wait()

    def factor(k, carry):
        above, back = carry
        below = jnp.where((k + 1).astype(F32) < kmt, vd[k], 0.0)
        whole = 1.0 / (1.0 + below + above - above * back)
        inv[k] = whole
        gain[k] = above * whole
        back = below * whole
        back_ref[k] = back
        return below, back

    lax.fori_loop(0, 64, factor, (zero, zero), unroll=16)

    for load in loads[6:]:
        load.wait()

    def hold(keys, loads):
        for v in range(16):
            key_ref[8 * v : 8 * v + 8, :] = keys[v]
            load_ref[8 * v : 8 * v + 8, :] = loads[v]

    def held(ref):
        return [ref[8 * v : 8 * v + 8, :] for v in range(16)]

    keys, shares = [], []
    for l in range(4):
        for j in range(4):
            rows = slice(8 * j, 8 * j + 8)
            place = (8 * j + sub8) * 128 + lane8
            keys.append((owner_ref[l, rows, :] << 23) | (cell_ref[l, rows, :] << 12) | place)
            shares.append(weight_ref[l, rows, :])
    hold(*merges(keys, shares, range(1, FIRST_MERGES + 1)))

    finish()

    mirror = jnp.where(is_top, 127 - lane8, lane8)

    def ghost_rows(north, south, fields):
        for base, dst in fields:
            for g in range(8):
                rows = slice(base + 8 * g, base + 8 * g + 8)
                put_rows(lanes_of(north[rows, :], mirror), dst, g, 40)
                put_rows(south[rows, :], dst, g, 7)

    def ghost_cols(from_west, from_east):
        edge[0:32, :] = jnp.where(odd, at_lane(from_east, 126), from_west)
        edge[32:64, :] = at_lane(jnp.where(odd, from_west, from_east), 127)

    ghost_rows(g_north, g_south, ((0, tp), (64, sp)))
    for g in range(8):
        put_rows(g_south[136 + 8 * g : 144 + 8 * g, :], vp, g, 7)
    kp[40:48, :] = lanes_of(g_north[128:136, :], mirror)
    kp[0:8, :] = g_south[128:136, :]
    ghost_cols(g_west[64:96, :], g_east[0:32, :])
    edge[64:96, :] = jnp.where(odd, at_lane(g_east[32:64, :], 126), g_west[32:64, :])
    edge[96:128, :] = g_west[96:128, :]

    first, last = lane == 0, lane == 127
    kmt_edge = edge[64:96, :]
    wet_east = jnp.minimum(kmt, jnp.where(last, kmt_edge, at_lane(kmt, 127)))
    wet_west = jnp.minimum(kmt, jnp.where(first, kmt_edge, at_lane(kmt, 1)))
    wet_north = jnp.minimum(kmt, kp[9:41, :])
    wet_south = jnp.minimum(kmt, kp[7:39, :])

    def stencil(src, row, k, turn, coefs):
        mid, east, west, north, south = coefs
        here = src[k, 8:40, :]
        ghost = at_lane(edge[row : row + 32, :], turn)
        on_east = jnp.where(last, ghost, at_lane(here, 127))
        on_west = jnp.where(first, ghost, at_lane(here, 1))
        return (
            mid * here + east * on_east + west * on_west
            + north * src[k, 9:41, :] + south * src[k, 7:39, :]
        )

    def advance(k, carry, turn, coefs):
        above = gain[k]
        ft = stencil(tp, 0, k, turn, coefs) + above * carry[0]
        fs = stencil(sp, 32, k, turn, coefs) + above * carry[1]
        t_ref[k] = ft
        s_ref[k] = fs
        return ft, fs

    def down_first(k, carry):
        turn = lax.rem(128 - 2 * k, 128)
        level = k.astype(F32)
        whole = inv[k]
        half_e = 0.5 * up[k]
        half_w = jnp.where(first, 0.5 * at_lane(edge[96:128, :], turn), at_lane(half_e, 1))
        half_n = 0.5 * vp[k, 8:40, :]
        half_s = 0.5 * vp[k, 7:39, :]
        on_e, on_w = level < wet_east, level < wet_west
        on_n, on_s = level < wet_north, level < wet_south
        east = jnp.where(on_e, mixing - half_e, 0.0)
        west = jnp.where(on_w, mixing + half_w, 0.0)
        north = jnp.where(on_n, mixing - half_n, 0.0)
        south = jnp.where(on_s, mixing + half_s, 0.0)
        faces = (
            jnp.where(on_e, 2 * mixing, 0.0) + jnp.where(on_w, 2 * mixing, 0.0)
        ) + (jnp.where(on_n, 2 * mixing, 0.0) + jnp.where(on_s, 2 * mixing, 0.0))
        mid = (1.0 + (((east + west) + (north + south)) - faces)) * whole
        east, west, north, south = east * whole, west * whole, north * whole, south * whole
        c_mid[k], c_east[k], c_west[k], c_north[k], c_south[k] = mid, east, west, north, south
        return advance(k, carry, turn, (mid, east, west, north, south))

    lax.fori_loop(0, 64, down_first, (zero, zero), unroll=32)

    def up_first(i, carry):
        xt, xs, pack_t, pack_s = carry
        k = 63 - i
        back = back_ref[k]
        xt = t_ref[k] + back * xt
        xs = s_ref[k] + back * xs
        tp[k, 8:40, :] = xt
        sp[k, 8:40, :] = xs
        pair = (lane >> 1) == k
        pack_t = jnp.where(pair, at_lane(xt, 2 * k + 1), pack_t)
        pack_s = jnp.where(pair, at_lane(xs, 2 * k + 1), pack_s)
        return xt, xs, pack_t, pack_s

    _, _, pack_t, pack_s = lax.fori_loop(0, 64, up_first, (zero, zero, zero, zero), unroll=32)
    col_out2[0:32, :] = to_west_cols(pack_t, pack_s)
    col_out2[32:64, :] = to_east_cols(pack_t, pack_s)
    for base, src in ((0, tp), (64, sp)):
        take_rows(src, 39, row_up2, base)
        take_rows(src, 8, row_down2, base)

    start, finish = exchange(
        4, 128, 128, 128, 64, 32,
        (row_up2, row_down2, col_out2), (g_north2, g_south2, g_west2, g_east2),
    )
    start()

    keys, shares = merges(held(key_ref), held(load_ref), range(FIRST_MERGES + 1, 15))
    hold(keys, shares)
    begin = owner_starts(keys)
    cells = owner_slots([((k >> 12) & 2047).astype(F32) for k in keys], begin)
    for c in range(4):
        send_cells[:, c, :] = jnp.concatenate(cells[c], axis=0).T

    pl.semaphore_wait(ready, n_lon - 1)

    def send_cell(d):
        to = lax.rem(me + d, n)
        pltpu.make_async_remote_copy(
            src_ref=send_cells.at[to], dst_ref=recv_cells.at[d], send_sem=cells_send,
            recv_sem=cells_recv,
            device_id=(to // n_lon, lax.rem(to, n_lon)), device_id_type=MESH,
        ).start()

    lax.fori_loop(1, n, lambda d, _: (send_cell(d), 0)[1], 0)

    finish()
    ghost_rows(g_north2, g_south2, ((0, tp), (64, sp)))
    ghost_cols(g_west2[32:64, :], g_east2[0:32, :])

    def down_second(k, carry):
        turn = lax.rem(128 - 2 * k, 128)
        return advance(k, carry, turn, (c_mid[k], c_east[k], c_west[k], c_north[k], c_south[k]))

    lax.fori_loop(0, 64, down_second, (zero, zero), unroll=32)

    def up_second(i, carry):
        k = 63 - i
        back = back_ref[k]
        xt = t_ref[k] + back * carry[0]
        xs = s_ref[k] + back * carry[1]
        t_ref[k] = xt
        s_ref[k] = xs
        return xt, xs

    xt, xs = lax.fori_loop(0, 64, up_second, (zero, zero), unroll=32)
    wet = jnp.where(kmt > 0.0, 1.0, 0.0)
    surf_ref[0] = xt * wet
    surf_ref[1] = xs * wet

    values = link_values(surf_ref, key_ref, load_ref)
    count = jnp.where(lane8 < 127, pltpu.roll(begin, 127, 1), 16384) - begin
    for f in range(2):
        slots = owner_slots(values[f], begin)
        for c in range(4):
            kept = [
                jnp.where(sub8 * 16 + (c * 128 + v) < count, slots[c][v], 0.0) for v in range(16)
            ]
            send[:, 4 * f + c, :] = jnp.concatenate(kept, axis=0).T

    def send_one(d, _):
        to = lax.rem(me + d, n)
        pltpu.make_async_remote_copy(
            src_ref=send.at[to], dst_ref=recv.at[d], send_sem=all_send,
            recv_sem=all_recv.at[d // GROUP],
            device_id=(to // n_lon, lax.rem(to, n_lon)), device_id_type=MESH,
        ).start()
        return 0

    lax.fori_loop(1, n, send_one, 0)
    recv[0] = send[me]
    recv_cells[0] = send_cells[me]
    got = recv_cells.at[1:n]
    pltpu.make_async_copy(got, got, cells_recv).wait()

    def add_group(g, total):
        @pl.when(g == 0)
        def _():
            part = recv.at[1:GROUP]
            pltpu.make_async_copy(part, part, all_recv.at[0]).wait()

        @pl.when(g > 0)
        def _():
            part = recv.at[pl.ds(pl.multiple_of(g * GROUP, GROUP), GROUP)]
            pltpu.make_async_copy(part, part, all_recv.at[g]).wait()

        left, right = group_operands(recv, recv_cells, g * GROUP)
        return total + lax.dot_general(
            right, left, (((1,), (1,)), ((), ())), preferred_element_type=F32
        )

    total = lax.fori_loop(0, n // GROUP, add_group, jnp.zeros((128, 64), F32))
    write_sums(total.T, atmo_ref)
    sent = send.at[0 : n - 1]
    pltpu.make_async_copy(sent, sent, all_send).wait()
    sent = send_cells.at[0 : n - 1]
    pltpu.make_async_copy(sent, sent, cells_send).wait()


def whole_call(n_lat, n_lon, *arrays):
    vm = pl.BlockSpec(memory_space=pltpu.VMEM)
    hbm = pl.BlockSpec(memory_space=pltpu.HBM)
    field = jax.ShapeDtypeStruct((64, 32, 128), F32)
    block, wide = pltpu.VMEM((64, 32, 128), F32), pltpu.VMEM((64, 48, 128), F32)
    links = pltpu.VMEM((4, 32, 128), I32)
    dma = pltpu.SemaphoreType.DMA
    n = n_lat * n_lon

    def rows(count, dtype=F32):
        return pltpu.VMEM((count, 128), dtype)

    return pl.pallas_call(
        functools.partial(whole_kernel, n_lat, n_lon),
        out_shape=(field, field, jax.ShapeDtypeStruct((2, 2048), F32)),
        in_specs=[hbm] * 9,
        out_specs=(vm,) * 3,
        scratch_shapes=[wide] * 3
        + [block] * 10
        + [rows(r) for r in (200, 136, 128, 128, 128, 64)]
        + [rows(r) for r in (136, 200, 128, 64, 128, 128, 64, 32)]
        + [rows(128), rows(48), pltpu.VMEM((32, 128), I32), links, links, pltpu.VMEM((4, 32, 128), F32)]
        + [rows(128, I32), rows(128), pltpu.VMEM((2, 32, 128), F32)]
        + [pltpu.VMEM((128, 8, 128), F32)] * 2
        + [pltpu.VMEM((128, 4, 128), F32)] * 2
        + [dma((9,)), dma((8,)), dma((8,)), pltpu.SemaphoreType.REGULAR, dma, dma((n // GROUP,)), dma, dma],
        compiler_params=pltpu.CompilerParams(
            collective_id=1, has_side_effects=True, vmem_limit_bytes=VMEM_MB << 20
        ),
    )(*(pltpu.with_memory_space_constraint(a, pltpu.HBM) for a in arrays))


def hand_kernel(t_in, s_in, atmo_in, t_out, s_out, atmo_out, sem):
    puts = [
        pltpu.make_async_copy(src, dst, sem.at[i])
        for i, (src, dst) in enumerate(((t_in, t_out), (s_in, s_out), (atmo_in, atmo_out)))
    ]
    for put in puts:
        put.start()
    for put in puts:
        put.wait()


def hand_call(temp, salt, atmo):
    hbm = pl.BlockSpec(memory_space=pl.ANY)
    shapes = [jax.ShapeDtypeStruct(a.shape, a.dtype) for a in (temp, salt, atmo)]
    return pl.pallas_call(
        hand_kernel,
        out_shape=tuple(shapes),
        in_specs=[pl.BlockSpec(memory_space=pltpu.VMEM)] * 3,
        out_specs=(hbm,) * 3,
        scratch_shapes=[pltpu.SemaphoreType.DMA((3,))],
        compiler_params=pltpu.CompilerParams(vmem_limit_bytes=HAND_MB << 20),
    )(temp, salt, atmo)


def solution(mesh):
    n_lat, n_lon = mesh.shape["lat"], mesh.shape["lon"]
    level, flat = P(None, "lat", "lon"), P("lat", "lon")
    return jax.shard_map(
        lambda *a: hand_call(*whole_call(n_lat, n_lon, *a)),
        mesh=mesh,
        in_specs=(level,) * 5 + (flat,) + (level,) * 3,
        out_specs=(level, level, P(None, ("lat", "lon"))),
        check_vma=False,
    )
```

```python
import functools

import jax
import jax.numpy as jnp
from jax import lax
from jax.experimental import pallas as pl
from jax.experimental.pallas import tpu as pltpu
from jax.sharding import PartitionSpec as P

I32 = jnp.int32
F32 = jnp.float32
BF16 = jnp.bfloat16
MESH = pl.DeviceIdType.MESH
mixing = 0.1
GROUP = 16
FIRST_MERGES = 13
VMEM_MB = 32
HAND_MB = 8


def lanes_of(x, idx):
    return jnp.take_along_axis(x, idx, axis=1, mode="promise_in_bounds")


def owner_starts(keys):
    lane = lax.broadcasted_iota(I32, (8, 128), 1)
    first = jnp.broadcast_to(keys[0][0:1, :], (8, 128))
    bound = lane << 23
    count = jnp.zeros((8, 128), I32)
    for step in (128, 64, 32, 16, 8, 4, 2, 1):
        trial = count + step
        value = lanes_of(first, jnp.minimum(trial - 1, 127))
        fits = jnp.logical_and(trial <= 128, value < bound)
        count = jnp.where(fits, trial, count)
    column = jnp.maximum(count - 1, 0)
    within = jnp.zeros((8, 128), I32)
    for v in range(16):
        within = within + jnp.where(lanes_of(keys[v], column) < bound, 1, 0)
    within = jnp.broadcast_to(jnp.sum(within, axis=0, keepdims=True), (8, 128))
    return jnp.where(count > 0, column * 128 + within, 0)


def owner_slots(tiles, start):
    sub = lax.broadcasted_iota(I32, (8, 128), 0)
    column = start >> 7
    turn = start & 127
    x = []
    for c in range(5):
        idx = jnp.minimum(column + c, 127)
        x.append([lanes_of(tiles[v], idx) for v in range(16)])
    for n in (64, 32, 16):
        on = (turn & n) != 0
        a = n // 16
        low = sub < 8 - a
        rolled = [[pltpu.roll(t, 8 - a, 0) for t in row] for row in x]
        x = [
            [
                jnp.where(on, jnp.where(low, rolled[c][v], rolled[min(c + 1, 4)][v]), x[c][v])
                for v in range(16)
            ]
            for c in range(5)
        ]
    low = sub < 7
    for n in (8, 4, 2, 1):
        on = (turn & n) != 0
        rolled = [[pltpu.roll(row[v], 7, 0) for v in range(n)] for row in x]
        out = []
        for c in range(5 if n > 1 else 4):
            row = []
            for v in range(16):
                if v + n < 16:
                    moved = x[c][v + n]
                else:
                    moved = jnp.where(low, rolled[c][v + n - 16], rolled[min(c + 1, 4)][v + n - 16])
                row.append(jnp.where(on, moved, x[c][v]))
            out.append(row)
        x = out
    return x


def link_values(surf_ref, key_ref, load_ref):
    keys = [key_ref[pl.ds(8 * v, 8), :] for v in range(16)]
    lanes = [k & 127 for k in keys]
    rows = [(k >> 7) & 31 for k in keys]
    found = [[jnp.zeros((8, 128), F32)] * 16 for _ in range(2)]
    for r in range(32):
        table = [jnp.broadcast_to(surf_ref[f, r : r + 1, :], (8, 128)) for f in range(2)]
        for v in range(16):
            here = rows[v] == r
            for f in range(2):
                found[f][v] = jnp.where(here, lanes_of(table[f], lanes[v]), found[f][v])
    loads = [load_ref[pl.ds(8 * v, 8), :] for v in range(16)]
    return [[loads[v] * found[f][v] for v in range(16)] for f in range(2)]


def write_sums(total, out_ref):
    for f in range(2):
        summed = total[32 * f : 32 * f + 16] + total[32 * f + 16 : 32 * f + 32]
        for h in range(16):
            out_ref[f : f + 1, 128 * h : 128 * h + 128] = summed[h : h + 1]


def at_lane(x, shift):
    return pltpu.roll(x, shift, 1)


def group_operands(recv_ref, cell_ref, first):
    high_id = lax.broadcasted_iota(I32, (16, 128), 0).astype(F32).astype(BF16)
    low_id = lax.broadcasted_iota(I32, (128, 128), 0).astype(F32).astype(BF16)
    left, right = [], []
    for q in range(GROUP):
        cell = cell_ref[first + q]
        high = jnp.floor(cell * (1.0 / 128.0))
        low = cell - 128.0 * high
        values = recv_ref[first + q]
        coarse = values.astype(BF16).astype(F32)
        fine = values - coarse
        for c in range(4):
            hits = jnp.broadcast_to(high[c : c + 1], (16, 128)).astype(BF16) == high_id
            part = []
            for f in range(2):
                for piece in (coarse, fine):
                    row = jnp.broadcast_to(piece[4 * f + c : 4 * f + c + 1], (16, 128)).astype(BF16)
                    part.append(jnp.where(hits, row, jnp.zeros_like(row)))
            left.append(jnp.concatenate(part, axis=0))
            match = jnp.broadcast_to(low[c : c + 1], (128, 128)).astype(BF16) == low_id
            right.append(jnp.where(match, jnp.ones((128, 128), BF16), jnp.zeros((128, 128), BF16)))
    return jnp.concatenate(left, axis=1), jnp.concatenate(right, axis=1)


def merges(keys, loads, tops):
    lane = lax.broadcasted_iota(I32, (8, 128), 1)
    sub = lax.broadcasted_iota(I32, (8, 128), 0)

    def bit(b):
        if b < 4 or b >= 14:
            return None
        where = sub >> (b - 4) if b < 7 else lane >> (b - 7)
        return (where & 1) == 1

    for top in tops:
        for b in range(top - 1, -1, -1):
            down = bit(top)
            new_k, new_w = list(keys), list(loads)
            if b < 4:
                for v in range(16):
                    if (v >> b) & 1:
                        continue
                    u = v | (1 << b)
                    if top < 4 and (v >> top) & 1:
                        swap = keys[v] < keys[u]
                    else:
                        swap = keys[v] > keys[u]
                    if down is not None:
                        swap = jnp.logical_xor(swap, down)
                    new_k[v] = jnp.where(swap, keys[u], keys[v])
                    new_k[u] = jnp.where(swap, keys[v], keys[u])
                    new_w[v] = jnp.where(swap, loads[u], loads[v])
                    new_w[u] = jnp.where(swap, loads[v], loads[u])
            else:
                keep_max = bit(b) if down is None else jnp.logical_xor(bit(b), down)
                if b < 7:
                    idx, axis = sub ^ (1 << (b - 4)), 0
                else:
                    idx, axis = lane ^ (1 << (b - 7)), 1
                for v in range(16):
                    k, w = keys[v], loads[v]
                    pk = jnp.take_along_axis(k, idx, axis=axis, mode="promise_in_bounds")
                    pw = jnp.take_along_axis(w, idx, axis=axis, mode="promise_in_bounds")
                    take = jnp.logical_or(
                        jnp.logical_and(keep_max, pk > k),
                        jnp.logical_and(jnp.logical_not(keep_max), pk < k),
                    )
                    new_k[v] = jnp.where(take, pk, k)
                    new_w[v] = jnp.where(take, pw, w)
            keys, loads = new_k, new_w
    return keys, loads


def whole_kernel(
    n_lat, n_lon,
    temp_hbm, salt_hbm, east_hbm, north_hbm, vdiff_hbm, kmt_hbm, owner_hbm, cell_hbm, weight_hbm,
    t_ref, s_ref, atmo_ref,
    tp, sp, vp, up, vd, inv, gain, back_ref, c_mid, c_east, c_west, c_north, c_south,
    row_up, row_down, col_out, row_up2, row_down2, col_out2,
    g_north, g_south, g_west, g_east, g_north2, g_south2, g_west2, g_east2,
    edge, kp, kmt_ref, owner_ref, cell_ref, weight_ref, key_ref, load_ref, surf_ref, send, recv, send_cells, recv_cells,
    load_sem, send_sem, recv_sem, ready, all_send, all_recv, cells_send, cells_recv,
):
    n = n_lat * n_lon
    lat, lon = lax.axis_index("lat"), lax.axis_index("lon")
    me = lat * n_lon + lon
    is_top = lat == n_lat - 1
    has_south = lat > 0
    north_id = (jnp.where(is_top, lat, lat + 1), jnp.where(is_top, n_lon - 1 - lon, lon))
    south_id = (jnp.maximum(lat - 1, 0), lon)
    east_id = (lat, lax.rem(lon + 1, n_lon))
    west_id = (lat, lax.rem(lon + n_lon - 1, n_lon))

    loads = [
        pltpu.make_async_copy(src, dst, load_sem.at[i])
        for i, (src, dst) in enumerate(
            (
                (kmt_hbm, kmt_ref),
                (temp_hbm, tp.at[:, 8:40, :]),
                (salt_hbm, sp.at[:, 8:40, :]),
                (east_hbm, up),
                (north_hbm, vp.at[:, 8:40, :]),
                (vdiff_hbm, vd),
                (owner_hbm, owner_ref),
                (cell_hbm, cell_ref),
                (weight_hbm, weight_ref),
            )
        )
    ]
    for load in loads:
        load.start()

    barrier = pltpu.get_barrier_semaphore()

    def greet_row(sem):
        def one(d, _):
            peer = (lat, lax.rem(lon + d, n_lon))
            pl.semaphore_signal(sem, inc=1, device_id=peer, device_id_type=MESH)
            return 0

        lax.fori_loop(1, n_lon, one, 0)

    def greet_column(d, _):
        peer = (lax.rem(lat + d, n_lat), lon)
        pl.semaphore_signal(barrier, inc=1, device_id=peer, device_id_type=MESH)
        return 0

    lax.fori_loop(1, n_lat, greet_column, 0)
    greet_row(barrier)

    @pl.when(jnp.logical_not(has_south))
    def _():
        g_south[...] = jnp.zeros_like(g_south)
        g_south2[...] = jnp.zeros_like(g_south2)

    lane = lax.broadcasted_iota(I32, (32, 128), 1)
    lane8 = lax.broadcasted_iota(I32, (8, 128), 1)
    sub8 = lax.broadcasted_iota(I32, (8, 128), 0)
    loads[0].wait()
    kmt = kmt_ref[...].astype(F32)
    kp[8:40, :] = kmt

    def take_rows(src, row, dst, base):
        for g in range(8):
            dst[base + 8 * g : base + 8 * g + 8, :] = src[8 * g : 8 * g + 8, row, :]

    def put_rows(value, dst, g, row):
        dst[8 * g : 8 * g + 8, row, :] = value

    for load in loads[1:5]:
        load.wait()
    for base, src in ((0, tp), (64, sp), (136, vp)):
        take_rows(src, 39, row_up, base)
    for base, src in ((0, tp), (64, sp)):
        take_rows(src, 8, row_down, base)
    row_up[128:136, :] = jnp.broadcast_to(kp[39:40, :], (8, 128))
    row_down[128:136, :] = jnp.broadcast_to(kp[8:9, :], (8, 128))

    def pack_level(k, packs):
        pair = (lane >> 1) == k
        fields = (tp[k, 8:40, :], sp[k, 8:40, :], up[k])
        return tuple(
            jnp.where(pair, at_lane(x, 2 * k + 1), p) for x, p in zip(fields, packs)
        )

    zero = jnp.zeros((32, 128), F32)
    packs = lax.fori_loop(0, 64, pack_level, (zero, zero, zero), unroll=32)
    odd = (lane & 1) == 1

    def to_west_cols(pack_t, pack_s):
        return jnp.where(odd, pack_t, at_lane(pack_s, 127))

    def to_east_cols(pack_t, pack_s):
        return jnp.where(odd, at_lane(pack_s, 1), pack_t)

    col_out[0:32, :] = to_west_cols(packs[0], packs[1])
    col_out[32:64, :] = at_lane(kmt, 1)
    col_out[64:96, :] = to_east_cols(packs[0], packs[1])
    col_out[96:128, :] = packs[2]

    pl.semaphore_wait(barrier, n_lat + n_lon - 2)

    def exchange(base, up_rows, top_rows, down_rows, east_rows, west_rows, bufs, ghosts):
        row_n, row_s, col = bufs
        north, south, west, east = ghosts

        def copy(src, dst, which, slot, peer):
            return pltpu.make_async_remote_copy(
                src_ref=src, dst_ref=dst, send_sem=send_sem.at[base + which],
                recv_sem=recv_sem.at[base + slot], device_id=peer, device_id_type=MESH,
            )

        to_north = copy(row_n.at[0:up_rows], south.at[0:up_rows], 0, 1, north_id)
        over_fold = copy(row_n.at[0:top_rows], north.at[0:top_rows], 0, 0, north_id)
        to_south = copy(row_s.at[0:down_rows], north.at[0:down_rows], 1, 0, south_id)
        to_east = copy(col.at[32:east_rows], west.at[32:east_rows], 2, 2, east_id)
        to_west = copy(col.at[0:west_rows], east.at[0:west_rows], 3, 3, west_id)

        def start_rows():
            @pl.when(is_top)
            def _():
                over_fold.start()

            @pl.when(jnp.logical_not(is_top))
            def _():
                to_north.start()

            @pl.when(has_south)
            def _():
                to_south.start()

        def start_cols():
            to_east.start()
            to_west.start()

        def finish():
            @pl.when(is_top)
            def _():
                over_fold.wait_send()

            @pl.when(jnp.logical_not(is_top))
            def _():
                to_north.wait_send()

            @pl.when(has_south)
            def _():
                to_south.wait_send()
                to_north.wait_recv()

            to_south.wait_recv()
            to_east.wait()
            to_west.wait()

        return start_rows, start_cols, finish

    start_rows, start_cols, finish = exchange(
        0, 200, 136, 136, 128, 64, (row_up, row_down, col_out), (g_north, g_south, g_west, g_east)
    )
    start_rows()
    start_cols()
    greet_row(ready)

    loads[5].wait()

    def factor(k, carry):
        above, back = carry
        below = jnp.where((k + 1).astype(F32) < kmt, vd[k], 0.0)
        whole = 1.0 / (1.0 + below + above - above * back)
        inv[k] = whole
        gain[k] = above * whole
        back = below * whole
        back_ref[k] = back
        return below, back

    lax.fori_loop(0, 64, factor, (zero, zero), unroll=16)

    for load in loads[6:]:
        load.wait()

    def hold(keys, loads):
        for v in range(16):
            key_ref[8 * v : 8 * v + 8, :] = keys[v]
            load_ref[8 * v : 8 * v + 8, :] = loads[v]

    def held(ref):
        return [ref[8 * v : 8 * v + 8, :] for v in range(16)]

    keys, shares = [], []
    for l in range(4):
        for j in range(4):
            rows = slice(8 * j, 8 * j + 8)
            place = (8 * j + sub8) * 128 + lane8
            keys.append((owner_ref[l, rows, :] << 23) | (cell_ref[l, rows, :] << 12) | place)
            shares.append(weight_ref[l, rows, :])
    hold(*merges(keys, shares, range(1, FIRST_MERGES + 1)))

    finish()

    mirror = jnp.where(is_top, 127 - lane8, lane8)

    def ghost_rows(north, south, fields):
        for base, dst in fields:
            for g in range(8):
                rows = slice(base + 8 * g, base + 8 * g + 8)
                put_rows(lanes_of(north[rows, :], mirror), dst, g, 40)
                put_rows(south[rows, :], dst, g, 7)

    def ghost_cols(from_west, from_east):
        edge[0:32, :] = jnp.where(odd, at_lane(from_east, 126), from_west)
        edge[32:64, :] = at_lane(jnp.where(odd, from_west, from_east), 127)

    ghost_rows(g_north, g_south, ((0, tp), (64, sp)))
    for g in range(8):
        put_rows(g_south[136 + 8 * g : 144 + 8 * g, :], vp, g, 7)
    kp[40:48, :] = lanes_of(g_north[128:136, :], mirror)
    kp[0:8, :] = g_south[128:136, :]
    ghost_cols(g_west[64:96, :], g_east[0:32, :])
    edge[64:96, :] = jnp.where(odd, at_lane(g_east[32:64, :], 126), g_west[32:64, :])
    edge[96:128, :] = g_west[96:128, :]

    first, last = lane == 0, lane == 127
    kmt_edge = edge[64:96, :]
    wet_east = jnp.minimum(kmt, jnp.where(last, kmt_edge, at_lane(kmt, 127)))
    wet_west = jnp.minimum(kmt, jnp.where(first, kmt_edge, at_lane(kmt, 1)))
    wet_north = jnp.minimum(kmt, kp[9:41, :])
    wet_south = jnp.minimum(kmt, kp[7:39, :])

    def stencil(src, row, k, turn, coefs):
        mid, east, west, north, south = coefs
        here = src[k, 8:40, :]
        ghost = at_lane(edge[row : row + 32, :], turn)
        on_east = jnp.where(last, ghost, at_lane(here, 127))
        on_west = jnp.where(first, ghost, at_lane(here, 1))
        return (
            mid * here + east * on_east + west * on_west
            + north * src[k, 9:41, :] + south * src[k, 7:39, :]
        )

    def advance(k, carry, turn, coefs):
        above = gain[k]
        ft = stencil(tp, 0, k, turn, coefs) + above * carry[0]
        fs = stencil(sp, 32, k, turn, coefs) + above * carry[1]
        t_ref[k] = ft
        s_ref[k] = fs
        return ft, fs

    def down_first(k, carry):
        turn = lax.rem(128 - 2 * k, 128)
        level = k.astype(F32)
        whole = inv[k]
        half_e = 0.5 * up[k]
        half_w = jnp.where(first, 0.5 * at_lane(edge[96:128, :], turn), at_lane(half_e, 1))
        half_n = 0.5 * vp[k, 8:40, :]
        half_s = 0.5 * vp[k, 7:39, :]
        on_e, on_w = level < wet_east, level < wet_west
        on_n, on_s = level < wet_north, level < wet_south
        east = jnp.where(on_e, mixing - half_e, 0.0)
        west = jnp.where(on_w, mixing + half_w, 0.0)
        north = jnp.where(on_n, mixing - half_n, 0.0)
        south = jnp.where(on_s, mixing + half_s, 0.0)
        faces = (
            jnp.where(on_e, 2 * mixing, 0.0) + jnp.where(on_w, 2 * mixing, 0.0)
        ) + (jnp.where(on_n, 2 * mixing, 0.0) + jnp.where(on_s, 2 * mixing, 0.0))
        mid = (1.0 + (((east + west) + (north + south)) - faces)) * whole
        east, west, north, south = east * whole, west * whole, north * whole, south * whole
        c_mid[k], c_east[k], c_west[k], c_north[k], c_south[k] = mid, east, west, north, south
        return advance(k, carry, turn, (mid, east, west, north, south))

    lax.fori_loop(0, 64, down_first, (zero, zero), unroll=32)

    def up_first(i, carry):
        xt, xs, pack_t, pack_s = carry
        k = 63 - i
        back = back_ref[k]
        xt = t_ref[k] + back * xt
        xs = s_ref[k] + back * xs
        tp[k, 8:40, :] = xt
        sp[k, 8:40, :] = xs
        pair = (lane >> 1) == k
        pack_t = jnp.where(pair, at_lane(xt, 2 * k + 1), pack_t)
        pack_s = jnp.where(pair, at_lane(xs, 2 * k + 1), pack_s)
        return xt, xs, pack_t, pack_s

    _, _, pack_t, pack_s = lax.fori_loop(0, 64, up_first, (zero, zero, zero, zero), unroll=32)
    for base, src in ((0, tp), (64, sp)):
        take_rows(src, 39, row_up2, base)
        take_rows(src, 8, row_down2, base)

    start_rows, start_cols, finish = exchange(
        4, 128, 128, 128, 64, 32,
        (row_up2, row_down2, col_out2), (g_north2, g_south2, g_west2, g_east2),
    )
    start_rows()
    col_out2[0:32, :] = to_west_cols(pack_t, pack_s)
    col_out2[32:64, :] = to_east_cols(pack_t, pack_s)
    start_cols()

    keys, shares = merges(held(key_ref), held(load_ref), range(FIRST_MERGES + 1, 15))
    hold(keys, shares)
    begin = owner_starts(keys)
    cells = owner_slots([((k >> 12) & 2047).astype(F32) for k in keys], begin)
    for c in range(4):
        send_cells[:, c, :] = jnp.concatenate(cells[c], axis=0).T

    pl.semaphore_wait(ready, n_lon - 1)

    def send_cell(d):
        to = lax.rem(me + d, n)
        pltpu.make_async_remote_copy(
            src_ref=send_cells.at[to], dst_ref=recv_cells.at[d], send_sem=cells_send,
            recv_sem=cells_recv,
            device_id=(to // n_lon, lax.rem(to, n_lon)), device_id_type=MESH,
        ).start()

    lax.fori_loop(1, n, lambda d, _: (send_cell(d), 0)[1], 0)

    finish()
    ghost_rows(g_north2, g_south2, ((0, tp), (64, sp)))
    ghost_cols(g_west2[32:64, :], g_east2[0:32, :])

    def down_second(k, carry):
        turn = lax.rem(128 - 2 * k, 128)
        return advance(k, carry, turn, (c_mid[k], c_east[k], c_west[k], c_north[k], c_south[k]))

    lax.fori_loop(0, 64, down_second, (zero, zero), unroll=32)

    def up_second(i, carry):
        k = 63 - i
        back = back_ref[k]
        xt = t_ref[k] + back * carry[0]
        xs = s_ref[k] + back * carry[1]
        t_ref[k] = xt
        s_ref[k] = xs
        return xt, xs

    xt, xs = lax.fori_loop(0, 64, up_second, (zero, zero), unroll=32)
    wet = jnp.where(kmt > 0.0, 1.0, 0.0)
    surf_ref[0] = xt * wet
    surf_ref[1] = xs * wet

    values = link_values(surf_ref, key_ref, load_ref)
    count = jnp.where(lane8 < 127, pltpu.roll(begin, 127, 1), 16384) - begin
    for f in range(2):
        slots = owner_slots(values[f], begin)
        for c in range(4):
            kept = [
                jnp.where(sub8 * 16 + (c * 128 + v) < count, slots[c][v], 0.0) for v in range(16)
            ]
            send[:, 4 * f + c, :] = jnp.concatenate(kept, axis=0).T

    def send_one(d, _):
        to = lax.rem(me + d, n)
        pltpu.make_async_remote_copy(
            src_ref=send.at[to], dst_ref=recv.at[d], send_sem=all_send,
            recv_sem=all_recv.at[d // GROUP],
            device_id=(to // n_lon, lax.rem(to, n_lon)), device_id_type=MESH,
        ).start()
        return 0

    lax.fori_loop(1, n, send_one, 0)
    recv[0] = send[me]
    recv_cells[0] = send_cells[me]
    got = recv_cells.at[1:n]
    pltpu.make_async_copy(got, got, cells_recv).wait()

    def add_group(g, total):
        @pl.when(g == 0)
        def _():
            part = recv.at[1:GROUP]
            pltpu.make_async_copy(part, part, all_recv.at[0]).wait()

        @pl.when(g > 0)
        def _():
            part = recv.at[pl.ds(pl.multiple_of(g * GROUP, GROUP), GROUP)]
            pltpu.make_async_copy(part, part, all_recv.at[g]).wait()

        left, right = group_operands(recv, recv_cells, g * GROUP)
        return total + lax.dot_general(
            right, left, (((1,), (1,)), ((), ())), preferred_element_type=F32
        )

    total = lax.fori_loop(0, n // GROUP, add_group, jnp.zeros((128, 64), F32))
    write_sums(total.T, atmo_ref)
    sent = send.at[0 : n - 1]
    pltpu.make_async_copy(sent, sent, all_send).wait()
    sent = send_cells.at[0 : n - 1]
    pltpu.make_async_copy(sent, sent, cells_send).wait()


def whole_call(n_lat, n_lon, *arrays):
    vm = pl.BlockSpec(memory_space=pltpu.VMEM)
    hbm = pl.BlockSpec(memory_space=pltpu.HBM)
    field = jax.ShapeDtypeStruct((64, 32, 128), F32)
    block, wide = pltpu.VMEM((64, 32, 128), F32), pltpu.VMEM((64, 48, 128), F32)
    links = pltpu.VMEM((4, 32, 128), I32)
    dma = pltpu.SemaphoreType.DMA
    n = n_lat * n_lon

    def rows(count, dtype=F32):
        return pltpu.VMEM((count, 128), dtype)

    return pl.pallas_call(
        functools.partial(whole_kernel, n_lat, n_lon),
        out_shape=(field, field, jax.ShapeDtypeStruct((2, 2048), F32)),
        in_specs=[hbm] * 9,
        out_specs=(vm,) * 3,
        scratch_shapes=[wide] * 3
        + [block] * 10
        + [rows(r) for r in (200, 136, 128, 128, 128, 64)]
        + [rows(r) for r in (136, 200, 128, 64, 128, 128, 64, 32)]
        + [rows(128), rows(48), pltpu.VMEM((32, 128), I32), links, links, pltpu.VMEM((4, 32, 128), F32)]
        + [rows(128, I32), rows(128), pltpu.VMEM((2, 32, 128), F32)]
        + [pltpu.VMEM((128, 8, 128), F32)] * 2
        + [pltpu.VMEM((128, 4, 128), F32)] * 2
        + [dma((9,)), dma((8,)), dma((8,)), pltpu.SemaphoreType.REGULAR, dma, dma((n // GROUP,)), dma, dma],
        compiler_params=pltpu.CompilerParams(
            collective_id=1, has_side_effects=True, vmem_limit_bytes=VMEM_MB << 20
        ),
    )(*(pltpu.with_memory_space_constraint(a, pltpu.HBM) for a in arrays))


def hand_kernel(t_in, s_in, atmo_in, t_out, s_out, atmo_out, sem):
    puts = [
        pltpu.make_async_copy(src, dst, sem.at[i])
        for i, (src, dst) in enumerate(((t_in, t_out), (s_in, s_out), (atmo_in, atmo_out)))
    ]
    for put in puts:
        put.start()
    for put in puts:
        put.wait()


def hand_call(temp, salt, atmo):
    hbm = pl.BlockSpec(memory_space=pl.ANY)
    shapes = [jax.ShapeDtypeStruct(a.shape, a.dtype) for a in (temp, salt, atmo)]
    return pl.pallas_call(
        hand_kernel,
        out_shape=tuple(shapes),
        in_specs=[pl.BlockSpec(memory_space=pltpu.VMEM)] * 3,
        out_specs=(hbm,) * 3,
        scratch_shapes=[pltpu.SemaphoreType.DMA((3,))],
        compiler_params=pltpu.CompilerParams(vmem_limit_bytes=HAND_MB << 20),
    )(temp, salt, atmo)


def solution(mesh):
    n_lat, n_lon = mesh.shape["lat"], mesh.shape["lon"]
    level, flat = P(None, "lat", "lon"), P("lat", "lon")
    return jax.shard_map(
        lambda *a: hand_call(*whole_call(n_lat, n_lon, *a)),
        mesh=mesh,
        in_specs=(level,) * 5 + (flat,) + (level,) * 3,
        out_specs=(level, level, P(None, ("lat", "lon"))),
        check_vma=False,
    )
```
